512 devices in a mesh: az: 32 (over x_lo, z), rg: 16 (over y, x_hi, core).
Axes of the slice: x: 4 (x_hi: 2, x_lo: 2; x = x_hi * 2 + x_lo), y: 4, z: 16, core: 2. Of those that a mesh axis runs over, the one named last changes fastest.
Arguments:
- raw_echo: bfloat16 [2, 32768, 6144], P(None, 'az', 'rg'), may hold values from -6 to 6
- range_chirp: bfloat16 [2, 512], replicated, may hold values from -0.1875 to 0.1875
- migration_taps: bfloat16 [8, 6144], P(None, 'rg'), may hold values from -2.09375 to 2.09375
- block_shift: int32 [48], P('rg'), may hold values from -60 to 60, as said below
- azimuth_chirp: bfloat16 [48, 2, 512], P('rg'), may hold values from -0.1875 to 0.1875
Outputs:
- focused_image: float32 [2, 32768, 6144], P(None, 'az', 'rg')
The draws below stay inside these ranges and needn't reach their ends.
Inputs may be any that keep to these rules, and one draw needn't show every extreme that they name: `block_shift`: every range block of 128 cells has one shift; the values -60 and 60 both occur in every draw.
All inputs are finite; a program needn't handle non-finite values.
Results may differ from the reference program's by a relative error of at most 0.0041.
Values may be sent and summed in bfloat16 or wider, within the bound.
A program may use at most 64 MiB of HBM per device.

```python
import jax
import jax.numpy as jnp
from jax import lax

AZ_DEV = 1024
RTAPS = 512
ATAPS = 512
TAPS = 8
MAXS = 60
BLK = 128
NA = 32768
NR = 6144
NRB = 48


def draw_block_shift(key, part):
    block_count = NR // BLK
    value_key = jax.random.fold_in(key, 11)
    order_key = jax.random.fold_in(key, 12)
    values = jax.random.randint(value_key, (block_count,), -MAXS, MAXS + 1, dtype=jnp.int32)
    placing = jax.random.permutation(order_key, block_count)
    values = values.at[placing[0]].set(-MAXS)
    return values.at[placing[1]].set(MAXS)


def levels(own_key, dims, split, low, largest):
    level = 1.0
    for axis_at, shards_of in split:
        steps = jax.random.uniform(jax.random.fold_in(jax.random.fold_in(own_key, 6), axis_at), (shards_of,), jnp.float32, low / len(split), largest / len(split))
        level = level * jnp.repeat(jnp.exp(steps), dims[axis_at] // shards_of).reshape((-1,) + (1,) * (len(dims) - 1 - axis_at))
    return level


def centred(key, extent, width, bound, shards=(), held_as=jnp.bfloat16):
    result = width * jax.random.normal(key, extent, jnp.float32)
    if shards:
        result = result * levels(key, extent, shards, -0.22, 0.18)
    return jnp.clip(result, -bound, bound).astype(held_as)


def setup_inputs(seed: int = 0) -> dict:
    keys = jax.random.split(jax.random.key(seed), 6)
    raw_echo = centred(keys[0], (2, NA, NR), 1.0, 6.0, ((1, 32), (2, 16)))
    range_chirp = centred(keys[1], (2, RTAPS), (2 * RTAPS) ** -0.5, 0.1875)
    migration_taps = centred(keys[2], (TAPS, NR), 0.35, 2.09375, ((1, 16),))
    block_shift = draw_block_shift(jax.random.fold_in(keys[5], 71), 0)
    azimuth_chirp = centred(keys[4], (NRB, 2, ATAPS), (2 * ATAPS) ** -0.5, 0.1875, ((0, 16),))
    return {"raw_echo": raw_echo, "range_chirp": range_chirp, "migration_taps": migration_taps, "block_shift": block_shift, "azimuth_chirp": azimuth_chirp}


def correlate(signal, tap_values):
    cell_total = signal.shape[-1]
    tap_count = tap_values.shape[0]
    length = cell_total + tap_count
    kernel = jnp.pad(jnp.conj(tap_values)[::-1], (0, length - tap_count))
    kernel = jnp.roll(kernel, -(tap_count // 2 - 1))
    spectrum = jnp.fft.fft(signal, n=length, axis=-1) * jnp.fft.fft(kernel)
    return jnp.fft.ifft(spectrum, axis=-1)[..., :cell_total]


def reference(raw_echo, range_chirp, migration_taps, block_shift, azimuth_chirp):
    margin = MAXS + TAPS // 2
    chirp_complex = range_chirp[0].astype(jnp.float32) + 1j * range_chirp[1].astype(jnp.float32)
    shift_cells = jnp.repeat(block_shift, BLK).astype(jnp.int32)
    cell_index = lax.iota(jnp.int32, NR)
    tap_float = migration_taps.astype(jnp.float32)

    def range_section(slab_index):
        slab_data = lax.dynamic_slice_in_dim(raw_echo, slab_index * AZ_DEV, AZ_DEV, 1).astype(jnp.float32)
        compressed = correlate(slab_data[0] + 1j * slab_data[1], chirp_complex)
        rounded = jnp.stack([compressed.real, compressed.imag]).astype(jnp.bfloat16)
        rounded = lax.optimization_barrier(rounded).astype(jnp.float32)
        padded = jnp.pad(rounded, ((0, 0), (0, 0), (margin, margin)))
        summed = jnp.zeros((2, AZ_DEV, NR), jnp.float32)
        for tap_index in range(TAPS):
            source = cell_index + margin + shift_cells + (tap_index - TAPS // 2)
            summed = summed + tap_float[tap_index] * jnp.take(padded, source, axis=2)
        return summed.astype(jnp.bfloat16)

    migrated = lax.map(range_section, lax.iota(jnp.int32, NA // AZ_DEV))
    migrated = jnp.transpose(migrated, (1, 0, 2, 3)).reshape(2, NA, NR)

    def azimuth_section(block_index):
        columns = lax.dynamic_slice_in_dim(migrated, block_index * BLK, BLK, 2).astype(jnp.float32)
        signal = jnp.transpose(columns[0] + 1j * columns[1])
        tap_pair = lax.dynamic_index_in_dim(azimuth_chirp, block_index, 0, keepdims=False).astype(jnp.float32)
        focused = jnp.transpose(correlate(signal, tap_pair[0] + 1j * tap_pair[1]))
        return jnp.stack([focused.real, focused.imag]).astype(jnp.float32)

    image_blocks = lax.map(azimuth_section, lax.iota(jnp.int32, NR // BLK))
    return jnp.transpose(image_blocks, (1, 2, 0, 3)).reshape(2, NA, NR)
```

```python
import functools

import jax
import jax.numpy as jnp
from jax import lax
from jax.experimental import pallas as pl
from jax.experimental.pallas import tpu as pltpu
from jax.sharding import PartitionSpec as P

MESH = pl.DeviceIdType.MESH
BLK = 128
HALF = 256
MAXS = 60
CHUNK = 128
BF16 = jnp.bfloat16
F32 = jnp.float32


def chunk_at(step, chunks):
    return jnp.where(step % 2 == 0, step // 2, chunks - 1 - step // 2)


def toeplitz_tiles(taps_row, front):
    zeros = jnp.zeros_like(taps_row)
    parts = [zeros, taps_row] if front else [taps_row, zeros]
    base = jnp.broadcast_to(jnp.concatenate(parts, axis=1), (BLK, 2 * taps_row.shape[1]))
    return pltpu.roll(base, 0, 1, stride=1, stride_axis=0)


def kernel(
    ranks, raw, chirp, taps, shift, azimuth, out,
    own, left, right, left_half, right_half, to_right, to_left,
    filters, toep, weights, azimuth_rows, migrated, total,
    own_sem, out_sem, range_send, range_recv, azimuth_send, azimuth_recv,
):
    az_count, rg_count = ranks
    az, rg = lax.axis_index("az"), lax.axis_index("rg")
    lines, cells = own.shape[1], own.shape[2]
    blocks = cells // BLK
    chunks = lines // CHUNK
    has_left, has_right = rg > 0, rg < rg_count - 1
    has_before, has_after = az > 0, az < az_count - 1
    to = {
        "left": (az, jnp.maximum(rg - 1, 0)),
        "right": (az, jnp.minimum(rg + 1, rg_count - 1)),
        "before": (jnp.maximum(az - 1, 0), rg),
        "after": (jnp.minimum(az + 1, az_count - 1), rg),
    }
    there = {"left": has_left, "right": has_right, "before": has_before, "after": has_after}

    load = pltpu.make_async_copy(raw, own, own_sem)
    load.start()

    barrier = pltpu.get_barrier_semaphore()
    count = 0
    for side, exists in there.items():
        @pl.when(exists)
        def _(side=side):
            pl.semaphore_signal(barrier, inc=1, device_id=to[side], device_id_type=MESH)
        count = count + jnp.where(exists, 1, 0)
    pl.semaphore_wait(barrier, count)

    def wide_copy(side, step):
        rows = pl.ds(pl.multiple_of(chunk_at(step, chunks) * CHUNK, CHUNK), CHUNK)
        direction = 0 if side == "right" else 1
        cols = pl.ds(cells - HALF, HALF) if side == "right" else pl.ds(0, HALF)
        return pltpu.make_async_remote_copy(
            src_ref=raw.at[:, rows, cols],
            dst_ref=(left if side == "right" else right).at[:, rows, :],
            send_sem=range_send.at[direction, 0, step],
            recv_sem=range_recv.at[direction, 0, step],
            device_id=to[side], device_id_type=MESH,
        )

    def half_copy(side, step):
        rows = pl.ds(pl.multiple_of(chunk_at(step, chunks) * CHUNK, CHUNK), CHUNK)
        direction = 0 if side == "right" else 1
        return pltpu.make_async_remote_copy(
            src_ref=(to_right if side == "right" else to_left).at[rows, :],
            dst_ref=(left_half if side == "right" else right_half).at[rows, :],
            send_sem=range_send.at[direction, 1, step],
            recv_sem=range_recv.at[direction, 1, step],
            device_id=to[side], device_id_type=MESH,
        )

    for side in ("right", "left"):
        @pl.when(there[side])
        def _(side=side):
            wide_copy(side, 0).start()

    load.wait()
    low = lax.broadcasted_iota(jnp.int32, (CHUNK, BLK), 1) < BLK // 2

    @pl.loop(0, chunks)
    def _(c):
        rows = pl.ds(pl.multiple_of(c * CHUNK, CHUNK), CHUNK)
        real, imag = own[0, rows, 0:BLK].astype(F32), own[1, rows, 0:BLK].astype(F32)
        to_right[rows, :] = jnp.where(low, pltpu.roll(real, BLK // 2, 1), imag).astype(BF16)
        real = own[0, rows, cells - BLK : cells].astype(F32)
        imag = own[1, rows, cells - BLK : cells].astype(F32)
        to_left[rows, :] = jnp.where(low, real, pltpu.roll(imag, BLK // 2, 1)).astype(BF16)

    @pl.loop(0, chunks)
    def _(step):
        for side in ("right", "left"):
            @pl.when(there[side])
            def _(side=side):
                @pl.when(step > 0)
                def _():
                    wide_copy(side, step).start()
                half_copy(side, step).start()

    @pl.when(jnp.logical_not(has_left))
    def _():
        left[...] = jnp.zeros_like(left)
        left_half[...] = jnp.zeros_like(left_half)

    @pl.when(jnp.logical_not(has_right))
    def _():
        right[...] = jnp.zeros_like(right)
        right_half[...] = jnp.zeros_like(right_half)

    @pl.when(jnp.logical_not(has_before))
    def _():
        migrated[0:HALF, :] = jnp.zeros((HALF, 2 * cells), BF16)

    @pl.when(jnp.logical_not(has_after))
    def _():
        migrated[HALF + lines :, :] = jnp.zeros((HALF, 2 * cells), BF16)

    total[...] = jnp.zeros_like(total)

    tap_count = taps.shape[0]
    row = lax.broadcasted_iota(jnp.int32, (2 * BLK, BLK), 0)
    column = lax.broadcasted_iota(jnp.int32, (2 * BLK, BLK), 1)
    toep[...] = jnp.zeros_like(toep)
    for part in range(2):
        rolled = toeplitz_tiles(chirp[part : part + 1, :].astype(F32), False)
        for d in range(5):
            tile = rolled[:, d * BLK : (d + 1) * BLK].T.astype(BF16)
            for p in range(2):
                u = d + p
                toep[part * 6 * BLK + u * BLK : part * 6 * BLK + (u + 1) * BLK, p * BLK : (p + 1) * BLK] = tile
    for b in range(blocks):
        offset = row - column - (shift[b] + MAXS)
        cell = rg * cells + b * BLK - BLK // 2 + row
        inside = jnp.logical_and(cell >= 0, cell < rg_count * cells)
        matrix = jnp.zeros((2 * BLK, BLK), F32)
        for k in range(tap_count):
            weight = jnp.broadcast_to(taps[k : k + 1, b * BLK : (b + 1) * BLK].astype(F32), matrix.shape)
            matrix = matrix + jnp.where(offset == k, weight, 0.0)
        matrix = jnp.where(inside, matrix, 0.0).astype(BF16)
        both = jnp.dot(toep[...], matrix, preferred_element_type=F32)
        real, imag = both[: 6 * BLK], both[6 * BLK :]
        filters[0] = jnp.concatenate([real, -imag], axis=1).astype(BF16)
        filters[1] = jnp.concatenate([imag, real], axis=1).astype(BF16)
        at = 0
        if b == 0:
            pieces = [(0, 64, 320), (1, 64, 320), (0, 320, 704), (1, 320, 704),
                      (0, 704, 768), None, (1, 704, 768), None, (0, 0, 64), (1, 0, 64)]
        elif b == 1:
            pieces = [None, (0, 0, 192), None, (1, 0, 192), (0, 192, 576), (1, 192, 576),
                      (0, 576, 768), None, (1, 576, 768), None]
        else:
            pieces = [None, (0, 0, 64), None, (1, 0, 64), (0, 64, 448), (1, 64, 448),
                      (0, 448, 704), (1, 448, 704), (0, 704, 768), (1, 704, 768)]
        for piece in pieces:
            if piece is None:
                weights[b, at : at + 64, :] = jnp.zeros((64, 2 * BLK), BF16)
                at += 64
            else:
                part, start, stop = piece
                weights[b, at : at + stop - start, :] = filters[part, start:stop, :]
                at += stop - start

    for b in range(blocks):
        for part in range(2):
            rolled = toeplitz_tiles(azimuth[b, part : part + 1, :].astype(F32), True).astype(BF16)
            for q in range(5):
                lane = (8 - q) % 8 * BLK
                azimuth_rows[b, q * BLK : (q + 1) * BLK, part * BLK : (part + 1) * BLK] = rolled[:, lane : lane + BLK]

    def turned(tile):
        real, imag = tile[:, :BLK], tile[:, BLK:]
        return jnp.concatenate([tile, jnp.concatenate([imag, -real], axis=1)], axis=0)

    def add_lines(source, first, count, target):
        for b in range(blocks):
            tile = turned(migrated[source, 2 * b * BLK : 2 * (b + 1) * BLK])
            result = jnp.dot(azimuth_rows[b, first : first + count, :], tile, preferred_element_type=F32)
            columns = slice(b * BLK, (b + 1) * BLK)
            total[0, target, columns] += result[:, :BLK]
            total[1, target, columns] += result[:, BLK:]

    def line_copy(step):
        up = step % 2 == 0
        c = chunk_at(step, chunks)
        source = pl.ds(pl.multiple_of(HALF + c * CHUNK, CHUNK), CHUNK)
        place = jnp.where(up, HALF + lines + step // 2 * CHUNK, CHUNK - step // 2 * CHUNK)
        place = pl.ds(pl.multiple_of(place, CHUNK), CHUNK)
        device = (jnp.where(up, to["before"][0], to["after"][0]), rg)
        return pltpu.make_async_remote_copy(
            src_ref=migrated.at[source, :],
            dst_ref=migrated.at[place, :],
            send_sem=azimuth_send.at[step], recv_sem=azimuth_recv.at[step],
            device_id=device, device_id_type=MESH,
        )

    @pl.loop(0, chunks)
    def _(step):
        c = chunk_at(step, chunks)
        rows = pl.ds(pl.multiple_of(c * CHUNK, CHUNK), CHUNK)

        @pl.when(step == chunks - 1)
        def _():
            for s in range(4):
                @pl.when(has_after if s % 2 == 0 else has_before)
                def _(s=s):
                    line_copy(s).wait_recv()
            add_lines(slice(0, 128), 512, 128, slice(256, 384))
            add_lines(slice(128, 256), 384, 256, slice(256, 512))
            add_lines(slice(HALF + lines, HALF + lines + 128), 0, 256, slice(lines, lines + 256))
            add_lines(slice(HALF + lines + 128, HALF + lines + 256), 0, 128, slice(lines + 128, lines + 256))

        for side, exists in (("right", has_left), ("left", has_right)):
            @pl.when(exists)
            def _(side=side):
                wide_copy(side, step).wait_recv()
                half_copy(side, step).wait_recv()

        own_parts = [own[0, rows, :], own[1, rows, :]]
        for b in range(blocks):
            if b == 0:
                parts = [left[0, rows, :], left[1, rows, :]] + own_parts + [
                    right[0, rows, :BLK], right[1, rows, :BLK], left_half[rows, :]]
            elif b == 1:
                parts = [left[0, rows, :], left[1, rows, :]] + own_parts + [right[0, rows, :], right[1, rows, :]]
            else:
                parts = [left[0, rows, BLK:], left[1, rows, BLK:]] + own_parts + [
                    right[0, rows, :], right[1, rows, :], right_half[rows, :]]
            joined = jnp.concatenate(parts, axis=1)
            depth = joined.shape[1]
            result = jnp.dot(joined, weights[b, :depth, :], preferred_element_type=F32)
            migrated[pl.ds(pl.multiple_of(HALF + c * CHUNK, CHUNK), CHUNK), 2 * b * BLK : 2 * (b + 1) * BLK] = result.astype(BF16)

        @pl.when(step < 4)
        def _():
            @pl.when(jnp.where(step % 2 == 0, has_before, has_after))
            def _():
                line_copy(step).start()

        add_lines(pl.ds(pl.multiple_of(HALF + c * CHUNK, CHUNK), CHUNK), 0, 5 * BLK,
                  pl.ds(pl.multiple_of(c * CHUNK, CHUNK), 5 * BLK))

    result_copy = pltpu.make_async_copy(total.at[:, pl.ds(HALF, lines), :], out, out_sem)
    result_copy.start()

    @pl.loop(0, chunks)
    def _(step):
        for side in ("right", "left"):
            @pl.when(there[side])
            def _(side=side):
                wide_copy(side, step).wait_send()
                half_copy(side, step).wait_send()

    for s in range(4):
        @pl.when(has_before if s % 2 == 0 else has_after)
        def _(s=s):
            line_copy(s).wait_send()
    result_copy.wait()


def per_device(ranks, raw_echo, range_chirp, migration_taps, block_shift, azimuth_chirp):
    lines, cells = raw_echo.shape[1:]
    blocks = cells // BLK
    chunks = lines // CHUNK
    vmem = pl.BlockSpec(memory_space=pltpu.VMEM)
    hbm = pl.BlockSpec(memory_space=pl.ANY)
    return pl.pallas_call(
        functools.partial(kernel, ranks),
        out_shape=jax.ShapeDtypeStruct((2, lines, cells), F32),
        in_specs=[hbm, vmem, vmem, pl.BlockSpec(memory_space=pltpu.SMEM), vmem],
        out_specs=hbm,
        scratch_shapes=[
            pltpu.VMEM((2, lines, cells), BF16),
            pltpu.VMEM((2, lines, HALF), BF16),
            pltpu.VMEM((2, lines, HALF), BF16),
            pltpu.VMEM((lines, BLK), BF16),
            pltpu.VMEM((lines, BLK), BF16),
            pltpu.VMEM((lines, BLK), BF16),
            pltpu.VMEM((lines, BLK), BF16),
            pltpu.VMEM((2, 6 * BLK, 2 * BLK), BF16),
            pltpu.VMEM((12 * BLK, 2 * BLK), BF16),
            pltpu.VMEM((blocks, 14 * BLK, 2 * BLK), BF16),
            pltpu.VMEM((blocks, 5 * BLK, 2 * BLK), BF16),
            pltpu.VMEM((lines + 2 * HALF, 2 * cells), BF16),
            pltpu.VMEM((2, lines + 2 * HALF, cells), F32),
            pltpu.SemaphoreType.DMA,
            pltpu.SemaphoreType.DMA,
            pltpu.SemaphoreType.DMA((2, 2, chunks)),
            pltpu.SemaphoreType.DMA((2, 2, chunks)),
            pltpu.SemaphoreType.DMA((4,)),
            pltpu.SemaphoreType.DMA((4,)),
        ],
        compiler_params=pltpu.CompilerParams(collective_id=0, has_side_effects=True),
        name="focus",
    )(raw_echo, range_chirp, migration_taps, block_shift, azimuth_chirp)


def solution(mesh):
    ranks = (mesh.shape["az"], mesh.shape["rg"])
    placed = (P(None, "az", "rg"), P(), P(None, "rg"), P("rg"), P("rg", None, None))
    return jax.shard_map(
        functools.partial(per_device, ranks), mesh=mesh, in_specs=placed, out_specs=P(None, "az", "rg"), check_vma=False
    )
```

```python
import functools

import jax
import jax.numpy as jnp
from jax import lax
from jax.experimental import pallas as pl
from jax.experimental.pallas import tpu as pltpu
from jax.sharding import PartitionSpec as P

MESH = pl.DeviceIdType.MESH
BLK = 128
HALF = 256
MAXS = 60
CHUNK = 128
BF16 = jnp.bfloat16
F32 = jnp.float32


def chunk_of(place, chunks):
    return jnp.where(place % 2 == 0, place // 2, chunks - 1 - place // 2)


def toeplitz_tiles(taps_row, front):
    zeros = jnp.zeros_like(taps_row)
    parts = [zeros, taps_row] if front else [taps_row, zeros]
    base = jnp.broadcast_to(jnp.concatenate(parts, axis=1), (BLK, 2 * taps_row.shape[1]))
    return pltpu.roll(base, 0, 1, stride=1, stride_axis=0)


def kernel(
    ranks, raw, chirp_in, taps_in, shift_in, azimuth_in, total, migrated, azimuth_rows,
    own, left, right, left_half, right_half, to_right, to_left, relay, relay_half, relay_lines,
    filters, toep, weights, chirp, taps, shift, azimuth,
    own_sem, small_sem, range_send, range_recv, azimuth_send, azimuth_recv,
    relay_send, relay_recv, lines_send, lines_recv, ready,
):
    az_count, rg_count = ranks
    az, rg = lax.axis_index("az"), lax.axis_index("rg")
    lines, cells = own.shape[1], own.shape[2]
    blocks = cells // BLK
    chunks = lines // CHUNK
    has_left, has_right = rg > 0, rg < rg_count - 1
    has_before, has_after = az > 0, az < az_count - 1
    to = {
        "left": (az, jnp.maximum(rg - 1, 0)),
        "right": (az, jnp.minimum(rg + 1, rg_count - 1)),
        "before": (jnp.maximum(az - 1, 0), rg),
        "after": (jnp.minimum(az + 1, az_count - 1), rg),
    }
    there = {"left": has_left, "right": has_right, "before": has_before, "after": has_after}
    row = max(rg_count // 4, 2)
    upper, lower, middle = row, rg_count - row - 1, az_count // 2
    passed = [] if az_count < 12 else [
        (1, 0, middle - 1, az_count - 2, middle),
        (1, 1, middle - 1, az_count - 3, middle),
        (3, 1, middle - 1, az_count - 4, middle),
        (0, 0, middle, middle - 2, middle - 1),
        (0, 1, middle, middle - 3, middle - 1),
        (2, 1, middle, middle - 4, middle - 1),
    ]
    opens, answers = az == middle, az == middle - 1
    first_rg, last_rg = rg == 0, rg == rg_count - 1
    near_first = jnp.logical_or(rg == upper, rg == upper - 1)
    near_last = jnp.logical_or(rg == lower, rg == lower + 1)
    both = [
        (to["left"], has_left), (to["right"], has_right),
        ((az, 0), near_first), ((az, rg_count - 1), near_last),
        ((az, jnp.where(first_rg, upper, lower)), jnp.logical_or(first_rg, last_rg)),
        ((az, jnp.where(first_rg, upper - 1, lower + 1)), jnp.logical_or(first_rg, last_rg)),
    ]
    greet = both + [
        (to["before"], has_before), (to["after"], jnp.logical_and(has_after, jnp.logical_not(answers))),
    ]
    expect = [exists for _, exists in both] + [jnp.logical_and(has_before, jnp.logical_not(opens)), has_after]
    answering = [answers]
    for _, _, source, via, target in passed:
        greet.append(((via, rg), opens))
        expect.append(az == via)
        if target == middle:
            greet.append(((source, rg), az == via))
            expect.append(az == source)
        else:
            greet.append(((via, rg), az == target))
            expect.append(az == via)
            answering.append(az == via)

    def place_at(step):
        early = jnp.where(step < 2, 2 * step + 1, 2 * step - 4)
        return jnp.where(jnp.logical_and(answers, step < 4), early, step)

    def chunk_at(step, chunks):
        return chunk_of(place_at(step), chunks)

    load = pltpu.make_async_copy(raw, own, own_sem)
    load.start()
    small = [
        pltpu.make_async_copy(source, place, small_sem.at[i])
        for i, (source, place) in enumerate(
            ((chirp_in, chirp), (taps_in, taps), (shift_in, shift), (azimuth_in, azimuth))
        )
    ]
    for copy in small:
        copy.start()

    barrier = pltpu.get_barrier_semaphore()
    count = 0
    for device, exists in greet:
        @pl.when(exists)
        def _(device=device):
            pl.semaphore_signal(barrier, inc=1, device_id=device, device_id_type=MESH)
    for exists in expect:
        count = count + jnp.where(exists, 1, 0)
    pl.semaphore_wait(barrier, count)
    for exists in answering:
        @pl.when(exists)
        def _():
            pl.semaphore_signal(ready, inc=1, device_id=(middle, rg), device_id_type=MESH)

    def wide_copy(side, step):
        rows = pl.ds(pl.multiple_of(chunk_at(step, chunks) * CHUNK, CHUNK), CHUNK)
        direction = 0 if side == "right" else 1
        cols = pl.ds(cells - HALF, HALF) if side == "right" else pl.ds(0, HALF)
        return pltpu.make_async_remote_copy(
            src_ref=raw.at[:, rows, cols],
            dst_ref=(left if side == "right" else right).at[:, rows, :],
            send_sem=range_send.at[direction, 0, step],
            recv_sem=range_recv.at[direction, 0, step],
            device_id=to[side], device_id_type=MESH,
        )

    def half_copy(side, step):
        rows = pl.ds(pl.multiple_of(chunk_at(step, chunks) * CHUNK, CHUNK), CHUNK)
        direction = 0 if side == "right" else 1
        return pltpu.make_async_remote_copy(
            src_ref=(to_right if side == "right" else to_left).at[rows, :],
            dst_ref=(left_half if side == "right" else right_half).at[rows, :],
            send_sem=range_send.at[direction, 1, step],
            recv_sem=range_recv.at[direction, 1, step],
            device_id=to[side], device_id_type=MESH,
        )

    def relayed(side, step):
        source = lower if side == "right" else upper
        return jnp.logical_and(rg == source, step % 2 == 0)

    def to_relay(side, step, piece):
        rows = pl.ds(pl.multiple_of(chunk_at(step, chunks) * CHUNK, CHUNK), CHUNK)
        direction = 0 if side == "right" else 1
        cols = pl.ds(cells - HALF, HALF) if side == "right" else pl.ds(0, HALF)
        device = (az, rg_count - 1 if side == "right" else 0)
        if piece == 0:
            return pltpu.make_async_remote_copy(
                src_ref=raw.at[:, rows, cols], dst_ref=relay.at[:, rows, :],
                send_sem=range_send.at[direction, 0, step], recv_sem=relay_recv.at[0, step],
                device_id=device, device_id_type=MESH,
            )
        return pltpu.make_async_remote_copy(
            src_ref=(to_right if side == "right" else to_left).at[rows, :], dst_ref=relay_half.at[rows, :],
            send_sem=range_send.at[direction, 1, step], recv_sem=relay_recv.at[1, step],
            device_id=device, device_id_type=MESH,
        )

    def from_relay(side, step, piece):
        rows = pl.ds(pl.multiple_of(chunk_at(step, chunks) * CHUNK, CHUNK), CHUNK)
        direction = 0 if side == "right" else 1
        device = (az, lower + 1 if side == "right" else upper - 1)
        if piece == 0:
            return pltpu.make_async_remote_copy(
                src_ref=relay.at[:, rows, :], dst_ref=(left if side == "right" else right).at[:, rows, :],
                send_sem=relay_send.at[0, step], recv_sem=range_recv.at[direction, 0, step],
                device_id=device, device_id_type=MESH,
            )
        return pltpu.make_async_remote_copy(
            src_ref=relay_half.at[rows, :], dst_ref=(left_half if side == "right" else right_half).at[rows, :],
            send_sem=relay_send.at[1, step], recv_sem=range_recv.at[direction, 1, step],
            device_id=device, device_id_type=MESH,
        )

    def send_wide(side, step):
        @pl.when(jnp.logical_and(there[side], jnp.logical_not(relayed(side, step))))
        def _():
            wide_copy(side, step).start()

        @pl.when(relayed(side, step))
        def _():
            to_relay(side, step, 0).start()

    def send_half(side, step):
        @pl.when(jnp.logical_and(there[side], jnp.logical_not(relayed(side, step))))
        def _():
            half_copy(side, step).start()

        @pl.when(relayed(side, step))
        def _():
            to_relay(side, step, 1).start()

    for side in ("right", "left"):
        send_wide(side, 0)

    load.wait()
    low = lax.broadcasted_iota(jnp.int32, (CHUNK, BLK), 1) < BLK // 2

    @pl.loop(0, chunks)
    def _(c):
        rows = pl.ds(pl.multiple_of(c * CHUNK, CHUNK), CHUNK)
        real, imag = own[0, rows, 0:BLK].astype(F32), own[1, rows, 0:BLK].astype(F32)
        to_right[rows, :] = jnp.where(low, pltpu.roll(real, BLK // 2, 1), imag).astype(BF16)
        real = own[0, rows, cells - BLK : cells].astype(F32)
        imag = own[1, rows, cells - BLK : cells].astype(F32)
        to_left[rows, :] = jnp.where(low, real, pltpu.roll(imag, BLK // 2, 1)).astype(BF16)

    @pl.loop(0, chunks)
    def _(step):
        for side in ("right", "left"):
            @pl.when(step > 0)
            def _(side=side):
                send_wide(side, step)
            send_half(side, step)

    @pl.when(jnp.logical_not(has_left))
    def _():
        left[...] = jnp.zeros_like(left)
        left_half[...] = jnp.zeros_like(left_half)

    @pl.when(jnp.logical_not(has_right))
    def _():
        right[...] = jnp.zeros_like(right)
        right_half[...] = jnp.zeros_like(right_half)

    @pl.when(jnp.logical_not(has_before))
    def _():
        migrated[0:HALF, :] = jnp.zeros((HALF, 2 * cells), BF16)

    @pl.when(jnp.logical_not(has_after))
    def _():
        migrated[HALF + lines :, :] = jnp.zeros((HALF, 2 * cells), BF16)

    total[...] = jnp.zeros_like(total)

    for copy in small:
        copy.wait()

    tap_count = taps.shape[0]
    row = lax.broadcasted_iota(jnp.int32, (2 * BLK, BLK), 0)
    column = lax.broadcasted_iota(jnp.int32, (2 * BLK, BLK), 1)
    toep[...] = jnp.zeros_like(toep)
    for part in range(2):
        rolled = toeplitz_tiles(chirp[part : part + 1, :].astype(F32), False)
        for d in range(5):
            tile = rolled[:, d * BLK : (d + 1) * BLK].T.astype(BF16)
            for p in range(2):
                u = d + p
                toep[part * 6 * BLK + u * BLK : part * 6 * BLK + (u + 1) * BLK, p * BLK : (p + 1) * BLK] = tile
    for b in range(blocks):
        offset = row - column - (shift[b] + MAXS)
        cell = rg * cells + b * BLK - BLK // 2 + row
        inside = jnp.logical_and(cell >= 0, cell < rg_count * cells)
        matrix = jnp.zeros((2 * BLK, BLK), F32)
        for k in range(tap_count):
            weight = jnp.broadcast_to(taps[k : k + 1, b * BLK : (b + 1) * BLK].astype(F32), matrix.shape)
            matrix = matrix + jnp.where(offset == k, weight, 0.0)
        matrix = jnp.where(inside, matrix, 0.0).astype(BF16)
        both = jnp.dot(toep[...], matrix, preferred_element_type=F32)
        real, imag = both[: 6 * BLK], both[6 * BLK :]
        filters[0] = jnp.concatenate([real, -imag], axis=1).astype(BF16)
        filters[1] = jnp.concatenate([imag, real], axis=1).astype(BF16)
        at = 0
        if b == 0:
            pieces = [(0, 64, 320), (1, 64, 320), (0, 320, 704), (1, 320, 704),
                      (0, 704, 768), None, (1, 704, 768), None, (0, 0, 64), (1, 0, 64)]
        elif b == 1:
            pieces = [None, (0, 0, 192), None, (1, 0, 192), (0, 192, 576), (1, 192, 576),
                      (0, 576, 768), None, (1, 576, 768), None]
        else:
            pieces = [None, (0, 0, 64), None, (1, 0, 64), (0, 64, 448), (1, 64, 448),
                      (0, 448, 704), (1, 448, 704), (0, 704, 768), (1, 704, 768)]
        for piece in pieces:
            if piece is None:
                weights[b, at : at + 64, :] = jnp.zeros((64, 2 * BLK), BF16)
                at += 64
            else:
                part, start, stop = piece
                weights[b, at : at + stop - start, :] = filters[part, start:stop, :]
                at += stop - start

    for b in range(blocks):
        for part in range(2):
            rolled = toeplitz_tiles(azimuth[b, part : part + 1, :].astype(F32), True).astype(BF16)
            for q in range(5):
                lane = (8 - q) % 8 * BLK
                azimuth_rows[b, q * BLK : (q + 1) * BLK, part * BLK : (part + 1) * BLK] = rolled[:, lane : lane + BLK]

    def turned(tile):
        real, imag = tile[:, :BLK], tile[:, BLK:]
        return jnp.concatenate([tile, jnp.concatenate([imag, -real], axis=1)], axis=0)

    def add_lines(source, first, count, target):
        for b in range(blocks):
            tile = turned(migrated[source, 2 * b * BLK : 2 * (b + 1) * BLK])
            result = jnp.dot(azimuth_rows[b, first : first + count, :], tile, preferred_element_type=F32)
            columns = slice(b * BLK, (b + 1) * BLK)
            total[0, target, columns] += result[:, :BLK]
            total[1, target, columns] += result[:, BLK:]

    def line_source(step, half):
        start = HALF + chunk_of(step, chunks) * CHUNK + half * (CHUNK // 2)
        return migrated.at[pl.ds(pl.multiple_of(start, CHUNK // 2), CHUNK // 2), :]

    def line_target(step, half):
        start = jnp.where(step % 2 == 0, HALF + lines + step // 2 * CHUNK, CHUNK - step // 2 * CHUNK)
        return migrated.at[pl.ds(pl.multiple_of(start + half * (CHUNK // 2), CHUNK // 2), CHUNK // 2), :]

    def is_passed(step, half):
        found = jnp.bool_(False)
        for at_step, at_half, source, _, target in passed:
            if at_half == half and target == middle:
                found = jnp.logical_or(found, jnp.logical_and(az == source, step == at_step))
        return found

    def line_to_relay(entry):
        step, half, _, via, _ = entry
        return pltpu.make_async_remote_copy(
            src_ref=line_source(step, half), dst_ref=relay_lines,
            send_sem=azimuth_send.at[step, half], recv_sem=lines_recv,
            device_id=(via, rg), device_id_type=MESH,
        )

    def line_from_relay(entry):
        step, half, _, _, target = entry
        return pltpu.make_async_remote_copy(
            src_ref=relay_lines, dst_ref=line_target(step, half),
            send_sem=lines_send, recv_sem=azimuth_recv.at[step, half],
            device_id=(target, rg), device_id_type=MESH,
        )

    def line_copy(step, half):
        device = (jnp.where(step % 2 == 0, to["before"][0], to["after"][0]), rg)
        return pltpu.make_async_remote_copy(
            src_ref=line_source(step, half), dst_ref=line_target(step, half),
            send_sem=azimuth_send.at[step, half], recv_sem=azimuth_recv.at[step, half],
            device_id=device, device_id_type=MESH,
        )

    @pl.loop(0, chunks)
    def _(step):
        c = chunk_at(step, chunks)
        rows = pl.ds(pl.multiple_of(c * CHUNK, CHUNK), CHUNK)

        @pl.when(step == chunks - 1)
        def _():
            for s in range(4):
                @pl.when(has_after if s % 2 == 0 else has_before)
                def _(s=s):
                    for half in range(2):
                        line_copy(s, half).wait_recv()
            add_lines(slice(0, 128), 512, 128, slice(256, 384))
            add_lines(slice(128, 256), 384, 256, slice(256, 512))
            add_lines(slice(HALF + lines, HALF + lines + 128), 0, 256, slice(lines, lines + 256))
            add_lines(slice(HALF + lines + 128, HALF + lines + 256), 0, 128, slice(lines + 128, lines + 256))

        for side, exists in (("left", first_rg), ("right", last_rg)):
            @pl.when(jnp.logical_and(exists, step % 2 == 0))
            def _(side=side):
                for piece in range(2):
                    to_relay(side, step, piece).wait_recv()
                    from_relay(side, step, piece).start()

        for entry in passed:
            @pl.when(jnp.logical_and(az == entry[3], step == (4 if entry[0] != 1 else 3)))
            def _(entry=entry):
                line_to_relay(entry).wait_recv()
                line_from_relay(entry).start()

        for side, exists in (("right", has_left), ("left", has_right)):
            @pl.when(exists)
            def _(side=side):
                wide_copy(side, step).wait_recv()
                half_copy(side, step).wait_recv()

        own_parts = [own[0, rows, :], own[1, rows, :]]
        for b in range(blocks):
            if b == 0:
                parts = [left[0, rows, :], left[1, rows, :]] + own_parts + [
                    right[0, rows, :BLK], right[1, rows, :BLK], left_half[rows, :]]
            elif b == 1:
                parts = [left[0, rows, :], left[1, rows, :]] + own_parts + [right[0, rows, :], right[1, rows, :]]
            else:
                parts = [left[0, rows, BLK:], left[1, rows, BLK:]] + own_parts + [
                    right[0, rows, :], right[1, rows, :], right_half[rows, :]]
            joined = jnp.concatenate(parts, axis=1)
            depth = joined.shape[1]
            result = jnp.dot(joined, weights[b, :depth, :], preferred_element_type=F32)
            migrated[pl.ds(pl.multiple_of(HALF + c * CHUNK, CHUNK), CHUNK), 2 * b * BLK : 2 * (b + 1) * BLK] = result.astype(BF16)

        @pl.when(step < 4)
        def _():
            place = place_at(step)
            exists = jnp.where(place % 2 == 0, jnp.logical_and(has_before, jnp.logical_not(opens)), has_after)
            for half in range(2):
                @pl.when(jnp.logical_and(exists, jnp.logical_not(is_passed(place, half))))
                def _(half=half):
                    line_copy(place, half).start()
            for entry in passed:
                if entry[4] == middle:
                    @pl.when(jnp.logical_and(az == entry[2], place == entry[0]))
                    def _(entry=entry):
                        line_to_relay(entry).start()

        @pl.when(jnp.logical_and(opens, step == 4))
        def _():
            pl.semaphore_wait(ready, len(answering))
            through = {(entry[0], entry[1]): entry for entry in passed if entry[2] == middle}
            for s in (0, 2):
                for half in range(2):
                    if (s, half) in through:
                        line_to_relay(through[s, half]).start()
                    else:
                        line_copy(s, half).start()

        @pl.when(step < chunks - 1)
        def _():
            add_lines(pl.ds(pl.multiple_of(HALF + c * CHUNK, CHUNK), CHUNK), 0, 5 * BLK,
                      pl.ds(pl.multiple_of(c * CHUNK, CHUNK), 5 * BLK))

    @pl.loop(0, chunks)
    def _(step):
        for side in ("right", "left"):
            @pl.when(there[side])
            def _(side=side):
                wide_copy(side, step).wait_send()
                half_copy(side, step).wait_send()

    for s in range(4):
        @pl.when(has_before if s % 2 == 0 else has_after)
        def _(s=s):
            for half in range(2):
                line_copy(s, half).wait_send()

    @pl.loop(0, chunks // 2)
    def _(pair):
        for side, exists in (("left", first_rg), ("right", last_rg)):
            @pl.when(exists)
            def _(side=side):
                for piece in range(2):
                    from_relay(side, 2 * pair, piece).wait_send()

    for entry in passed:
        @pl.when(az == entry[3])
        def _(entry=entry):
            line_from_relay(entry).wait_send()


def finish(total, lines_in, azimuth_rows, out, stage, sems):
    lines, blocks = out.shape[1], azimuth_rows.shape[0]
    last = lines // 2
    start, stop = last - HALF, last + CHUNK + HALF
    copies = [
        pltpu.make_async_copy(total.at[:, HALF : HALF + start, :], out.at[:, 0:start, :], sems.at[0]),
        pltpu.make_async_copy(total.at[:, HALF + stop : HALF + lines, :], out.at[:, stop:lines, :], sems.at[1]),
    ]
    for copy in copies:
        copy.start()
    tiles = []
    for b in range(blocks):
        tile = lines_in[HALF + last : HALF + last + CHUNK, 2 * b * BLK : 2 * (b + 1) * BLK]
        real, imag = tile[:, :BLK], tile[:, BLK:]
        tiles.append(jnp.concatenate([tile, jnp.concatenate([imag, -real], axis=1)], axis=0))
    at = 0
    for piece, rows in enumerate((256, 256, 128)):
        for b in range(blocks):
            result = jnp.dot(azimuth_rows[b, at : at + rows, :], tiles[b], preferred_element_type=F32)
            columns = slice(b * BLK, (b + 1) * BLK)
            source = slice(HALF + start + at, HALF + start + at + rows)
            stage[0, at : at + rows, columns] = total[0, source, columns] + result[:, :BLK]
            stage[1, at : at + rows, columns] = total[1, source, columns] + result[:, BLK:]
        copy = pltpu.make_async_copy(
            stage.at[:, at : at + rows, :], out.at[:, start + at : start + at + rows, :], sems.at[2 + piece]
        )
        copy.start()
        copies.append(copy)
        at += rows
    for copy in copies:
        copy.wait()


def per_device(ranks, raw_echo, range_chirp, migration_taps, block_shift, azimuth_chirp):
    lines, cells = raw_echo.shape[1:]
    blocks = cells // BLK
    chunks = lines // CHUNK
    vmem = pl.BlockSpec(memory_space=pltpu.VMEM)
    hbm = pl.BlockSpec(memory_space=pltpu.HBM)
    total, migrated, azimuth_rows = pl.pallas_call(
        functools.partial(kernel, ranks),
        out_shape=(
            pltpu.VMEM((2, lines + 2 * HALF, cells), F32),
            pltpu.VMEM((lines + 2 * HALF, 2 * cells), BF16),
            pltpu.VMEM((blocks, 5 * BLK, 2 * BLK), BF16),
        ),
        in_specs=[hbm] * 5,
        out_specs=(vmem, vmem, vmem),
        scratch_shapes=[
            pltpu.VMEM((2, lines, cells), BF16),
            pltpu.VMEM((2, lines, HALF), BF16),
            pltpu.VMEM((2, lines, HALF), BF16),
            pltpu.VMEM((lines, BLK), BF16),
            pltpu.VMEM((lines, BLK), BF16),
            pltpu.VMEM((lines, BLK), BF16),
            pltpu.VMEM((lines, BLK), BF16),
            pltpu.VMEM((2, lines, HALF), BF16),
            pltpu.VMEM((lines, BLK), BF16),
            pltpu.VMEM((CHUNK // 2, 2 * cells), BF16),
            pltpu.VMEM((2, 6 * BLK, 2 * BLK), BF16),
            pltpu.VMEM((12 * BLK, 2 * BLK), BF16),
            pltpu.VMEM((blocks, 14 * BLK, 2 * BLK), BF16),
            pltpu.VMEM(range_chirp.shape, BF16),
            pltpu.VMEM(migration_taps.shape, BF16),
            pltpu.SMEM(block_shift.shape, jnp.int32),
            pltpu.VMEM(azimuth_chirp.shape, BF16),
            pltpu.SemaphoreType.DMA,
            pltpu.SemaphoreType.DMA((4,)),
            pltpu.SemaphoreType.DMA((2, 2, chunks)),
            pltpu.SemaphoreType.DMA((2, 2, chunks)),
            pltpu.SemaphoreType.DMA((4, 2)),
            pltpu.SemaphoreType.DMA((4, 2)),
            pltpu.SemaphoreType.DMA((2, chunks)),
            pltpu.SemaphoreType.DMA((2, chunks)),
            pltpu.SemaphoreType.DMA,
            pltpu.SemaphoreType.DMA,
            pltpu.SemaphoreType.REGULAR,
        ],
        compiler_params=pltpu.CompilerParams(collective_id=0, has_side_effects=True, vmem_limit_bytes=40 << 20),
        name="focus",
    )(*(
        pltpu.with_memory_space_constraint(value, pltpu.HBM)
        for value in (raw_echo, range_chirp, migration_taps, block_shift, azimuth_chirp)
    ))
    return pl.pallas_call(
        finish,
        out_shape=jax.ShapeDtypeStruct((2, lines, cells), F32),
        in_specs=[vmem, vmem, vmem],
        out_specs=hbm,
        scratch_shapes=[
            pltpu.VMEM((2, 2 * HALF + CHUNK, cells), F32),
            pltpu.SemaphoreType.DMA((5,)),
        ],
        compiler_params=pltpu.CompilerParams(vmem_limit_bytes=40 << 20),
        name="finish",
    )(total, migrated, azimuth_rows)


def solution(mesh):
    ranks = (mesh.shape["az"], mesh.shape["rg"])
    placed = (P(None, "az", "rg"), P(), P(None, "rg"), P("rg"), P("rg", None, None))
    return jax.shard_map(
        functools.partial(per_device, ranks), mesh=mesh, in_specs=placed, out_specs=P(None, "az", "rg"), check_vma=False
    )
```

```python
import functools

import jax
import jax.numpy as jnp
from jax import lax
from jax.experimental import pallas as pl
from jax.experimental.pallas import tpu as pltpu
from jax.sharding import PartitionSpec as P

MESH = pl.DeviceIdType.MESH
BLK = 128
HALF = 256
MAXS = 60
CHUNK = 128
AHEAD = 3
BF16 = jnp.bfloat16
F32 = jnp.float32


def chunk_of(place, chunks):
    return jnp.where(place % 2 == 0, place // 2, chunks - 1 - place // 2)


def toeplitz_tiles(taps_row, front):
    zeros = jnp.zeros_like(taps_row)
    parts = [zeros, taps_row] if front else [taps_row, zeros]
    base = jnp.broadcast_to(jnp.concatenate(parts, axis=1), (BLK, 2 * taps_row.shape[1]))
    return pltpu.roll(base, 0, 1, stride=1, stride_axis=0)


def kernel(
    ranks, raw, chirp_in, taps_in, shift_in, azimuth_in, total, migrated, azimuth_rows,
    own, left, right, left_half, right_half, to_right, to_left, relay, relay_half, relay_lines,
    filters, toep, weights, chirp, taps, shift, azimuth,
    own_sem, small_sem, range_send, range_recv, azimuth_send, azimuth_recv,
    relay_send, relay_recv, lines_send, lines_recv, ready,
):
    az_count, rg_count = ranks
    az, rg = lax.axis_index("az"), lax.axis_index("rg")
    lines, cells = own.shape[1], own.shape[2]
    blocks = cells // BLK
    chunks = lines // CHUNK
    has_left, has_right = rg > 0, rg < rg_count - 1
    has_before, has_after = az > 0, az < az_count - 1
    to = {
        "left": (az, jnp.maximum(rg - 1, 0)),
        "right": (az, jnp.minimum(rg + 1, rg_count - 1)),
        "before": (jnp.maximum(az - 1, 0), rg),
        "after": (jnp.minimum(az + 1, az_count - 1), rg),
    }
    there = {"left": has_left, "right": has_right, "before": has_before, "after": has_after}
    width = 4 if rg_count >= 8 else 2
    heights = rg_count // width
    y, column_at = rg // width, rg % width
    first_column, last_column = column_at == 0, column_at == width - 1
    up, down = y > 0, y < heights - 1
    source = {"left": jnp.logical_and(first_column, up), "right": jnp.logical_and(last_column, down)}
    relaying = {"left": jnp.logical_and(first_column, down), "right": jnp.logical_and(last_column, up)}
    source_count = {"left": 2 * (heights - y), "right": 2 * (y + 1)}
    relay_count = {"left": 2 * (heights - y - 1), "right": 2 * y}
    middle = az_count // 2
    passed = [] if az_count < 12 else [
        (1, 0, middle - 1, az_count - 2, middle),
        (1, 1, middle - 1, az_count - 3, middle),
        (3, 1, middle - 1, az_count - 4, middle),
        (0, 0, middle, middle - 2, middle - 1),
        (0, 1, middle, middle - 3, middle - 1),
        (2, 1, middle, middle - 4, middle - 1),
    ]
    opens, answers = az == middle, az == middle - 1
    both = [
        (to["left"], has_left), (to["right"], has_right),
        ((az, jnp.maximum(rg - width, 0)), source["left"]),
        ((az, jnp.minimum(rg + width, rg_count - 1)), relaying["left"]),
        ((az, jnp.minimum(rg + width - 1, rg_count - 1)), relaying["left"]),
        ((az, jnp.maximum(rg - width + 1, 0)), source["right"]),
        ((az, jnp.minimum(rg + width, rg_count - 1)), source["right"]),
        ((az, jnp.maximum(rg - width, 0)), relaying["right"]),
        ((az, jnp.maximum(rg - width + 1, 0)), relaying["right"]),
        ((az, jnp.minimum(rg + width - 1, rg_count - 1)), source["left"]),
    ]
    greet = both + [
        (to["before"], has_before), (to["after"], jnp.logical_and(has_after, jnp.logical_not(answers))),
    ]
    expect = [exists for _, exists in both] + [jnp.logical_and(has_before, jnp.logical_not(opens)), has_after]
    answering = [answers]
    for _, _, sender, via, target in passed:
        greet.append(((via, rg), opens))
        expect.append(az == via)
        if target == middle:
            greet.append(((sender, rg), az == via))
            expect.append(az == sender)
        else:
            greet.append(((via, rg), az == target))
            expect.append(az == via)
            answering.append(az == via)

    def place_at(step):
        early = jnp.where(step < 2, 2 * step + 1, 2 * step - 4)
        return jnp.where(jnp.logical_and(answers, step < 4), early, step)

    def chunk_at(step, chunks):
        return chunk_of(place_at(step), chunks)

    load = pltpu.make_async_copy(raw, own, own_sem)
    load.start()
    small = [
        pltpu.make_async_copy(source, place, small_sem.at[i])
        for i, (source, place) in enumerate(
            ((chirp_in, chirp), (taps_in, taps), (shift_in, shift), (azimuth_in, azimuth))
        )
    ]
    for copy in small:
        copy.start()

    barrier = pltpu.get_barrier_semaphore()
    count = 0
    for device, exists in greet:
        @pl.when(exists)
        def _(device=device):
            pl.semaphore_signal(barrier, inc=1, device_id=device, device_id_type=MESH)
    for exists in expect:
        count = count + jnp.where(exists, 1, 0)
    pl.semaphore_wait(barrier, count)
    for exists in answering:
        @pl.when(exists)
        def _():
            pl.semaphore_signal(ready, inc=1, device_id=(middle, rg), device_id_type=MESH)

    def wide_copy(side, step):
        rows = pl.ds(pl.multiple_of(chunk_at(step, chunks) * CHUNK, CHUNK), CHUNK)
        direction = 0 if side == "right" else 1
        cols = pl.ds(cells - HALF, HALF) if side == "right" else pl.ds(0, HALF)
        return pltpu.make_async_remote_copy(
            src_ref=raw.at[:, rows, cols],
            dst_ref=(left if side == "right" else right).at[:, rows, :],
            send_sem=range_send.at[direction, 0, step],
            recv_sem=range_recv.at[direction, 0, step],
            device_id=to[side], device_id_type=MESH,
        )

    def half_copy(side, step):
        rows = pl.ds(pl.multiple_of(chunk_at(step, chunks) * CHUNK, CHUNK), CHUNK)
        direction = 0 if side == "right" else 1
        return pltpu.make_async_remote_copy(
            src_ref=(to_right if side == "right" else to_left).at[rows, :],
            dst_ref=(left_half if side == "right" else right_half).at[rows, :],
            send_sem=range_send.at[direction, 1, step],
            recv_sem=range_recv.at[direction, 1, step],
            device_id=to[side], device_id_type=MESH,
        )

    def relayed(side, step):
        return jnp.logical_and(source[side], step >= chunks - source_count[side])

    def to_relay(side, step, piece):
        rows = pl.ds(pl.multiple_of(chunk_at(step, chunks) * CHUNK, CHUNK), CHUNK)
        direction = 0 if side == "right" else 1
        cols = pl.ds(cells - HALF, HALF) if side == "right" else pl.ds(0, HALF)
        device = (az, jnp.minimum(rg + width, rg_count - 1) if side == "right" else jnp.maximum(rg - width, 0))
        if piece == 0:
            return pltpu.make_async_remote_copy(
                src_ref=raw.at[:, rows, cols], dst_ref=relay.at[:, rows, :],
                send_sem=range_send.at[direction, 0, step], recv_sem=relay_recv.at[0, step],
                device_id=device, device_id_type=MESH,
            )
        return pltpu.make_async_remote_copy(
            src_ref=(to_right if side == "right" else to_left).at[rows, :], dst_ref=relay_half.at[rows, :],
            send_sem=range_send.at[direction, 1, step], recv_sem=relay_recv.at[1, step],
            device_id=device, device_id_type=MESH,
        )

    def from_relay(side, step, piece):
        rows = pl.ds(pl.multiple_of(chunk_at(step, chunks) * CHUNK, CHUNK), CHUNK)
        direction = 0 if side == "right" else 1
        device = (az, jnp.maximum(rg - width + 1, 0) if side == "right" else jnp.minimum(rg + width - 1, rg_count - 1))
        if piece == 0:
            return pltpu.make_async_remote_copy(
                src_ref=relay.at[:, rows, :], dst_ref=(left if side == "right" else right).at[:, rows, :],
                send_sem=relay_send.at[0, step], recv_sem=range_recv.at[direction, 0, step],
                device_id=device, device_id_type=MESH,
            )
        return pltpu.make_async_remote_copy(
            src_ref=relay_half.at[rows, :], dst_ref=(left_half if side == "right" else right_half).at[rows, :],
            send_sem=relay_send.at[1, step], recv_sem=range_recv.at[direction, 1, step],
            device_id=device, device_id_type=MESH,
        )

    def send_wide(side, step):
        @pl.when(jnp.logical_and(there[side], jnp.logical_not(relayed(side, step))))
        def _():
            wide_copy(side, step).start()

        @pl.when(relayed(side, step))
        def _():
            to_relay(side, step, 0).start()

    def send_half(side, step):
        @pl.when(jnp.logical_and(there[side], jnp.logical_not(relayed(side, step))))
        def _():
            half_copy(side, step).start()

        @pl.when(relayed(side, step))
        def _():
            to_relay(side, step, 1).start()

    for side in ("right", "left"):
        send_wide(side, 0)

    load.wait()
    low = lax.broadcasted_iota(jnp.int32, (CHUNK, BLK), 1) < BLK // 2

    @pl.loop(0, chunks)
    def _(c):
        rows = pl.ds(pl.multiple_of(c * CHUNK, CHUNK), CHUNK)
        real, imag = own[0, rows, 0:BLK].astype(F32), own[1, rows, 0:BLK].astype(F32)
        to_right[rows, :] = jnp.where(low, pltpu.roll(real, BLK // 2, 1), imag).astype(BF16)
        real = own[0, rows, cells - BLK : cells].astype(F32)
        imag = own[1, rows, cells - BLK : cells].astype(F32)
        to_left[rows, :] = jnp.where(low, real, pltpu.roll(imag, BLK // 2, 1)).astype(BF16)

    @pl.loop(0, chunks)
    def _(step):
        for side in ("right", "left"):
            @pl.when(step > 0)
            def _(side=side):
                send_wide(side, step)
            send_half(side, step)

    @pl.when(jnp.logical_not(has_left))
    def _():
        left[...] = jnp.zeros_like(left)
        left_half[...] = jnp.zeros_like(left_half)

    @pl.when(jnp.logical_not(has_right))
    def _():
        right[...] = jnp.zeros_like(right)
        right_half[...] = jnp.zeros_like(right_half)

    @pl.when(jnp.logical_not(has_before))
    def _():
        migrated[0:HALF, :] = jnp.zeros((HALF, 2 * cells), BF16)

    @pl.when(jnp.logical_not(has_after))
    def _():
        migrated[HALF + lines :, :] = jnp.zeros((HALF, 2 * cells), BF16)

    total[...] = jnp.zeros_like(total)

    for copy in small:
        copy.wait()

    tap_count = taps.shape[0]
    row = lax.broadcasted_iota(jnp.int32, (2 * BLK, BLK), 0)
    column = lax.broadcasted_iota(jnp.int32, (2 * BLK, BLK), 1)
    toep[...] = jnp.zeros_like(toep)
    for part in range(2):
        rolled = toeplitz_tiles(chirp[part : part + 1, :].astype(F32), False)
        for d in range(5):
            tile = rolled[:, d * BLK : (d + 1) * BLK].T.astype(BF16)
            for p in range(2):
                u = d + p
                toep[part * 6 * BLK + u * BLK : part * 6 * BLK + (u + 1) * BLK, p * BLK : (p + 1) * BLK] = tile
    for b in range(blocks):
        offset = row - column - (shift[b] + MAXS)
        cell = rg * cells + b * BLK - BLK // 2 + row
        inside = jnp.logical_and(cell >= 0, cell < rg_count * cells)
        matrix = jnp.zeros((2 * BLK, BLK), F32)
        for k in range(tap_count):
            weight = jnp.broadcast_to(taps[k : k + 1, b * BLK : (b + 1) * BLK].astype(F32), matrix.shape)
            matrix = matrix + jnp.where(offset == k, weight, 0.0)
        matrix = jnp.where(inside, matrix, 0.0).astype(BF16)
        both = jnp.dot(toep[...], matrix, preferred_element_type=F32)
        real, imag = both[: 6 * BLK], both[6 * BLK :]
        filters[0] = jnp.concatenate([real, -imag], axis=1).astype(BF16)
        filters[1] = jnp.concatenate([imag, real], axis=1).astype(BF16)
        at = 0
        if b == 0:
            pieces = [(0, 64, 320), (1, 64, 320), (0, 320, 704), (1, 320, 704),
                      (0, 704, 768), None, (1, 704, 768), None, (0, 0, 64), (1, 0, 64)]
        elif b == 1:
            pieces = [None, (0, 0, 192), None, (1, 0, 192), (0, 192, 576), (1, 192, 576),
                      (0, 576, 768), None, (1, 576, 768), None]
        else:
            pieces = [None, (0, 0, 64), None, (1, 0, 64), (0, 64, 448), (1, 64, 448),
                      (0, 448, 704), (1, 448, 704), (0, 704, 768), (1, 704, 768)]
        for piece in pieces:
            if piece is None:
                weights[b, at : at + 64, :] = jnp.zeros((64, 2 * BLK), BF16)
                at += 64
            else:
                part, start, stop = piece
                weights[b, at : at + stop - start, :] = filters[part, start:stop, :]
                at += stop - start

    for b in range(blocks):
        for part in range(2):
            rolled = toeplitz_tiles(azimuth[b, part : part + 1, :].astype(F32), True).astype(BF16)
            for q in range(5):
                lane = (8 - q) % 8 * BLK
                azimuth_rows[b, q * BLK : (q + 1) * BLK, part * BLK : (part + 1) * BLK] = rolled[:, lane : lane + BLK]

    def turned(tile):
        real, imag = tile[:, :BLK], tile[:, BLK:]
        return jnp.concatenate([tile, jnp.concatenate([imag, -real], axis=1)], axis=0)

    def add_lines(source, first, count, target):
        for b in range(blocks):
            tile = turned(migrated[source, 2 * b * BLK : 2 * (b + 1) * BLK])
            result = jnp.dot(azimuth_rows[b, first : first + count, :], tile, preferred_element_type=F32)
            columns = slice(b * BLK, (b + 1) * BLK)
            total[0, target, columns] += result[:, :BLK]
            total[1, target, columns] += result[:, BLK:]

    def line_source(step, half):
        start = HALF + chunk_of(step, chunks) * CHUNK + half * (CHUNK // 2)
        return migrated.at[pl.ds(pl.multiple_of(start, CHUNK // 2), CHUNK // 2), :]

    def line_target(step, half):
        start = jnp.where(step % 2 == 0, HALF + lines + step // 2 * CHUNK, CHUNK - step // 2 * CHUNK)
        return migrated.at[pl.ds(pl.multiple_of(start + half * (CHUNK // 2), CHUNK // 2), CHUNK // 2), :]

    def is_passed(step, half):
        found = jnp.bool_(False)
        for at_step, at_half, sender, _, target in passed:
            if at_half == half and target == middle:
                found = jnp.logical_or(found, jnp.logical_and(az == sender, step == at_step))
        return found

    def line_to_relay(entry):
        step, half, _, via, _ = entry
        return pltpu.make_async_remote_copy(
            src_ref=line_source(step, half), dst_ref=relay_lines,
            send_sem=azimuth_send.at[step, half], recv_sem=lines_recv,
            device_id=(via, rg), device_id_type=MESH,
        )

    def line_from_relay(entry):
        step, half, _, _, target = entry
        return pltpu.make_async_remote_copy(
            src_ref=relay_lines, dst_ref=line_target(step, half),
            send_sem=lines_send, recv_sem=azimuth_recv.at[step, half],
            device_id=(target, rg), device_id_type=MESH,
        )

    def line_copy(step, half):
        device = (jnp.where(step % 2 == 0, to["before"][0], to["after"][0]), rg)
        return pltpu.make_async_remote_copy(
            src_ref=line_source(step, half), dst_ref=line_target(step, half),
            send_sem=azimuth_send.at[step, half], recv_sem=azimuth_recv.at[step, half],
            device_id=device, device_id_type=MESH,
        )

    @pl.loop(0, chunks)
    def _(step):
        c = chunk_at(step, chunks)
        rows = pl.ds(pl.multiple_of(c * CHUNK, CHUNK), CHUNK)

        @pl.when(step == chunks - 1)
        def _():
            for s in range(4):
                @pl.when(has_after if s % 2 == 0 else has_before)
                def _(s=s):
                    for half in range(2):
                        line_copy(s, half).wait_recv()
            add_lines(slice(0, 128), 512, 128, slice(256, 384))
            add_lines(slice(128, 256), 384, 256, slice(256, 512))
            add_lines(slice(HALF + lines, HALF + lines + 128), 0, 256, slice(lines, lines + 256))
            add_lines(slice(HALF + lines + 128, HALF + lines + 256), 0, 128, slice(lines + 128, lines + 256))

        for side in ("left", "right"):
            for late in (chunks - 2 * (heights - 1), step + AHEAD):
                first = isinstance(late, int)
                @pl.when(jnp.logical_and(
                    jnp.logical_and(relaying[side], late >= chunks - relay_count[side]),
                    step == 0 if first else late < chunks,
                ))
                def _(side=side, late=late):
                    for piece in range(2):
                        to_relay(side, late, piece).wait_recv()
                        from_relay(side, late, piece).start()

        for entry in passed:
            @pl.when(jnp.logical_and(az == entry[3], step == {1: 2, 3: 3}.get(entry[0], 4)))
            def _(entry=entry):
                line_to_relay(entry).wait_recv()
                line_from_relay(entry).start()

        for side, exists in (("right", has_left), ("left", has_right)):
            @pl.when(exists)
            def _(side=side):
                wide_copy(side, step).wait_recv()
                half_copy(side, step).wait_recv()

        own_parts = [own[0, rows, :], own[1, rows, :]]
        for b in range(blocks):
            if b == 0:
                parts = [left[0, rows, :], left[1, rows, :]] + own_parts + [
                    right[0, rows, :BLK], right[1, rows, :BLK], left_half[rows, :]]
            elif b == 1:
                parts = [left[0, rows, :], left[1, rows, :]] + own_parts + [right[0, rows, :], right[1, rows, :]]
            else:
                parts = [left[0, rows, BLK:], left[1, rows, BLK:]] + own_parts + [
                    right[0, rows, :], right[1, rows, :], right_half[rows, :]]
            joined = jnp.concatenate(parts, axis=1)
            depth = joined.shape[1]
            result = jnp.dot(joined, weights[b, :depth, :], preferred_element_type=F32)
            migrated[pl.ds(pl.multiple_of(HALF + c * CHUNK, CHUNK), CHUNK), 2 * b * BLK : 2 * (b + 1) * BLK] = result.astype(BF16)

        @pl.when(step < 4)
        def _():
            place = place_at(step)
            exists = jnp.where(place % 2 == 0, jnp.logical_and(has_before, jnp.logical_not(opens)), has_after)
            for half in range(2):
                @pl.when(jnp.logical_and(exists, jnp.logical_not(is_passed(place, half))))
                def _(half=half):
                    line_copy(place, half).start()
            for entry in passed:
                if entry[4] == middle:
                    @pl.when(jnp.logical_and(az == entry[2], place == entry[0]))
                    def _(entry=entry):
                        line_to_relay(entry).start()

        @pl.when(jnp.logical_and(opens, step == 4))
        def _():
            pl.semaphore_wait(ready, len(answering))
            through = {(entry[0], entry[1]): entry for entry in passed if entry[2] == middle}
            for s in (0, 2):
                for half in range(2):
                    if (s, half) in through:
                        line_to_relay(through[s, half]).start()
                    else:
                        line_copy(s, half).start()

        @pl.when(step < chunks - 1)
        def _():
            add_lines(pl.ds(pl.multiple_of(HALF + c * CHUNK, CHUNK), CHUNK), 0, 5 * BLK,
                      pl.ds(pl.multiple_of(c * CHUNK, CHUNK), 5 * BLK))

    @pl.loop(0, chunks)
    def _(step):
        for side in ("right", "left"):
            @pl.when(there[side])
            def _(side=side):
                wide_copy(side, step).wait_send()
                half_copy(side, step).wait_send()

    for s in range(4):
        @pl.when(has_before if s % 2 == 0 else has_after)
        def _(s=s):
            for half in range(2):
                line_copy(s, half).wait_send()

    @pl.loop(0, chunks)
    def _(step):
        for side in ("left", "right"):
            @pl.when(jnp.logical_and(relaying[side], step >= chunks - relay_count[side]))
            def _(side=side):
                for piece in range(2):
                    from_relay(side, step, piece).wait_send()

    for entry in passed:
        @pl.when(az == entry[3])
        def _(entry=entry):
            line_from_relay(entry).wait_send()


def finish(total, lines_in, azimuth_rows, out, stage, sems):
    lines, blocks = out.shape[1], azimuth_rows.shape[0]
    last = lines // 2
    start, stop = last - HALF, last + CHUNK + HALF
    copies = [
        pltpu.make_async_copy(total.at[:, HALF : HALF + start, :], out.at[:, 0:start, :], sems.at[0]),
        pltpu.make_async_copy(total.at[:, HALF + stop : HALF + lines, :], out.at[:, stop:lines, :], sems.at[1]),
    ]
    for copy in copies:
        copy.start()
    tiles = []
    for b in range(blocks):
        tile = lines_in[HALF + last : HALF + last + CHUNK, 2 * b * BLK : 2 * (b + 1) * BLK]
        real, imag = tile[:, :BLK], tile[:, BLK:]
        tiles.append(jnp.concatenate([tile, jnp.concatenate([imag, -real], axis=1)], axis=0))
    at = 0
    for piece, rows in enumerate((256, 256, 128)):
        for b in range(blocks):
            result = jnp.dot(azimuth_rows[b, at : at + rows, :], tiles[b], preferred_element_type=F32)
            columns = slice(b * BLK, (b + 1) * BLK)
            source = slice(HALF + start + at, HALF + start + at + rows)
            stage[0, at : at + rows, columns] = total[0, source, columns] + result[:, :BLK]
            stage[1, at : at + rows, columns] = total[1, source, columns] + result[:, BLK:]
        copy = pltpu.make_async_copy(
            stage.at[:, at : at + rows, :], out.at[:, start + at : start + at + rows, :], sems.at[2 + piece]
        )
        copy.start()
        copies.append(copy)
        at += rows
    for copy in copies:
        copy.wait()


def per_device(ranks, raw_echo, range_chirp, migration_taps, block_shift, azimuth_chirp):
    lines, cells = raw_echo.shape[1:]
    blocks = cells // BLK
    chunks = lines // CHUNK
    vmem = pl.BlockSpec(memory_space=pltpu.VMEM)
    hbm = pl.BlockSpec(memory_space=pltpu.HBM)
    total, migrated, azimuth_rows = pl.pallas_call(
        functools.partial(kernel, ranks),
        out_shape=(
            pltpu.VMEM((2, lines + 2 * HALF, cells), F32),
            pltpu.VMEM((lines + 2 * HALF, 2 * cells), BF16),
            pltpu.VMEM((blocks, 5 * BLK, 2 * BLK), BF16),
        ),
        in_specs=[hbm] * 5,
        out_specs=(vmem, vmem, vmem),
        scratch_shapes=[
            pltpu.VMEM((2, lines, cells), BF16),
            pltpu.VMEM((2, lines, HALF), BF16),
            pltpu.VMEM((2, lines, HALF), BF16),
            pltpu.VMEM((lines, BLK), BF16),
            pltpu.VMEM((lines, BLK), BF16),
            pltpu.VMEM((lines, BLK), BF16),
            pltpu.VMEM((lines, BLK), BF16),
            pltpu.VMEM((2, lines, HALF), BF16),
            pltpu.VMEM((lines, BLK), BF16),
            pltpu.VMEM((CHUNK // 2, 2 * cells), BF16),
            pltpu.VMEM((2, 6 * BLK, 2 * BLK), BF16),
            pltpu.VMEM((12 * BLK, 2 * BLK), BF16),
            pltpu.VMEM((blocks, 14 * BLK, 2 * BLK), BF16),
            pltpu.VMEM(range_chirp.shape, BF16),
            pltpu.VMEM(migration_taps.shape, BF16),
            pltpu.SMEM(block_shift.shape, jnp.int32),
            pltpu.VMEM(azimuth_chirp.shape, BF16),
            pltpu.SemaphoreType.DMA,
            pltpu.SemaphoreType.DMA((4,)),
            pltpu.SemaphoreType.DMA((2, 2, chunks)),
            pltpu.SemaphoreType.DMA((2, 2, chunks)),
            pltpu.SemaphoreType.DMA((4, 2)),
            pltpu.SemaphoreType.DMA((4, 2)),
            pltpu.SemaphoreType.DMA((2, chunks)),
            pltpu.SemaphoreType.DMA((2, chunks)),
            pltpu.SemaphoreType.DMA,
            pltpu.SemaphoreType.DMA,
            pltpu.SemaphoreType.REGULAR,
        ],
        compiler_params=pltpu.CompilerParams(collective_id=0, has_side_effects=True, vmem_limit_bytes=40 << 20),
        name="focus",
    )(*(
        pltpu.with_memory_space_constraint(value, pltpu.HBM)
        for value in (raw_echo, range_chirp, migration_taps, block_shift, azimuth_chirp)
    ))
    return pl.pallas_call(
        finish,
        out_shape=jax.ShapeDtypeStruct((2, lines, cells), F32),
        in_specs=[vmem, vmem, vmem],
        out_specs=hbm,
        scratch_shapes=[
            pltpu.VMEM((2, 2 * HALF + CHUNK, cells), F32),
            pltpu.SemaphoreType.DMA((5,)),
        ],
        compiler_params=pltpu.CompilerParams(vmem_limit_bytes=40 << 20),
        name="finish",
    )(total, migrated, azimuth_rows)


def solution(mesh):
    ranks = (mesh.shape["az"], mesh.shape["rg"])
    placed = (P(None, "az", "rg"), P(), P(None, "rg"), P("rg"), P("rg", None, None))
    return jax.shard_map(
        functools.partial(per_device, ranks), mesh=mesh, in_specs=placed, out_specs=P(None, "az", "rg"), check_vma=False
    )
```

```python
import functools

import jax
import jax.numpy as jnp
from jax import lax
from jax.experimental import pallas as pl
from jax.experimental.pallas import tpu as pltpu
from jax.sharding import PartitionSpec as P

MESH = pl.DeviceIdType.MESH
BLK = 128
HALF = 256
MAXS = 60
CHUNK = 128
AHEAD = 3
BF16 = jnp.bfloat16
F32 = jnp.float32


def chunk_of(place, chunks):
    return jnp.where(place % 2 == 0, place // 2, chunks - 1 - place // 2)


def toeplitz_tiles(taps_row, front):
    zeros = jnp.zeros_like(taps_row)
    parts = [zeros, taps_row] if front else [taps_row, zeros]
    base = jnp.broadcast_to(jnp.concatenate(parts, axis=1), (BLK, 2 * taps_row.shape[1]))
    return pltpu.roll(base, 0, 1, stride=1, stride_axis=0)


def kernel(
    ranks, raw, chirp_in, taps_in, shift_in, azimuth_in, total, migrated, azimuth_rows,
    own, left, right, left_half, right_half, to_right, to_left, relay, relay_half, relay_lines,
    filters, toep, weights, chirp, taps, shift, azimuth,
    own_sem, small_sem, range_send, range_recv, azimuth_send, azimuth_recv,
    relay_send, relay_recv, lines_send, lines_recv, ready,
):
    az_count, rg_count = ranks
    az, rg = lax.axis_index("az"), lax.axis_index("rg")
    lines, cells = own.shape[1], own.shape[2]
    blocks = cells // BLK
    chunks = lines // CHUNK
    has_left, has_right = rg > 0, rg < rg_count - 1
    has_before, has_after = az > 0, az < az_count - 1
    to = {
        "left": (az, jnp.maximum(rg - 1, 0)),
        "right": (az, jnp.minimum(rg + 1, rg_count - 1)),
        "before": (jnp.maximum(az - 1, 0), rg),
        "after": (jnp.minimum(az + 1, az_count - 1), rg),
    }
    there = {"left": has_left, "right": has_right, "before": has_before, "after": has_after}
    width = 4 if rg_count >= 8 else 2
    heights = rg_count // width
    y, column_at = rg // width, rg % width
    first_column, last_column = column_at == 0, column_at == width - 1
    up, down = y > 0, y < heights - 1
    source = {"left": jnp.logical_and(first_column, up), "right": jnp.logical_and(last_column, down)}
    relaying = {"left": jnp.logical_and(first_column, down), "right": jnp.logical_and(last_column, up)}
    source_count = {"left": 2 * (heights - y), "right": 2 * (y + 1)}
    relay_count = {"left": 2 * (heights - y - 1), "right": 2 * y}
    middle = az_count // 2
    passed = [] if az_count < 12 else [
        (1, 0, middle - 1, az_count - 2, middle),
        (1, 1, middle - 1, az_count - 3, middle),
        (3, 1, middle - 1, az_count - 4, middle),
        (3, 0, middle - 1, middle + 1, middle),
        (0, 0, middle, middle - 2, middle - 1),
        (0, 1, middle, middle - 3, middle - 1),
        (2, 1, middle, middle - 4, middle - 1),
    ]
    opens, answers = az == middle, az == middle - 1
    both = [
        (to["left"], has_left), (to["right"], has_right),
        ((az, jnp.maximum(rg - width, 0)), source["left"]),
        ((az, jnp.minimum(rg + width, rg_count - 1)), relaying["left"]),
        ((az, jnp.minimum(rg + width - 1, rg_count - 1)), relaying["left"]),
        ((az, jnp.maximum(rg - width + 1, 0)), source["right"]),
        ((az, jnp.minimum(rg + width, rg_count - 1)), source["right"]),
        ((az, jnp.maximum(rg - width, 0)), relaying["right"]),
        ((az, jnp.maximum(rg - width + 1, 0)), relaying["right"]),
        ((az, jnp.minimum(rg + width - 1, rg_count - 1)), source["left"]),
    ]
    greet = both + [
        (to["before"], has_before), (to["after"], jnp.logical_and(has_after, jnp.logical_not(answers))),
    ]
    expect = [exists for _, exists in both] + [jnp.logical_and(has_before, jnp.logical_not(opens)), has_after]
    answering = [answers]
    for _, _, sender, via, target in passed:
        greet.append(((via, rg), opens))
        expect.append(az == via)
        if target == middle:
            greet.append(((sender, rg), az == via))
            expect.append(az == sender)
        else:
            greet.append(((via, rg), az == target))
            expect.append(az == via)
            answering.append(az == via)

    def place_at(step):
        early = jnp.where(step < 2, 2 * step + 1, 2 * step - 4)
        return jnp.where(jnp.logical_and(answers, step < 4), early, step)

    def chunk_at(step, chunks):
        return chunk_of(place_at(step), chunks)

    load = pltpu.make_async_copy(raw, own, own_sem)
    load.start()
    small = [
        pltpu.make_async_copy(source, place, small_sem.at[i])
        for i, (source, place) in enumerate(
            ((chirp_in, chirp), (taps_in, taps), (shift_in, shift), (azimuth_in, azimuth))
        )
    ]
    for copy in small:
        copy.start()

    barrier = pltpu.get_barrier_semaphore()
    count = 0
    for device, exists in greet:
        @pl.when(exists)
        def _(device=device):
            pl.semaphore_signal(barrier, inc=1, device_id=device, device_id_type=MESH)
    for exists in expect:
        count = count + jnp.where(exists, 1, 0)
    pl.semaphore_wait(barrier, count)
    for exists in answering:
        @pl.when(exists)
        def _():
            pl.semaphore_signal(ready, inc=1, device_id=(middle, rg), device_id_type=MESH)

    def wide_copy(side, step):
        rows = pl.ds(pl.multiple_of(chunk_at(step, chunks) * CHUNK, CHUNK), CHUNK)
        direction = 0 if side == "right" else 1
        cols = pl.ds(cells - HALF, HALF) if side == "right" else pl.ds(0, HALF)
        return pltpu.make_async_remote_copy(
            src_ref=raw.at[:, rows, cols],
            dst_ref=(left if side == "right" else right).at[:, rows, :],
            send_sem=range_send.at[direction, 0, step],
            recv_sem=range_recv.at[direction, 0, step],
            device_id=to[side], device_id_type=MESH,
        )

    def half_copy(side, step):
        rows = pl.ds(pl.multiple_of(chunk_at(step, chunks) * CHUNK, CHUNK), CHUNK)
        direction = 0 if side == "right" else 1
        return pltpu.make_async_remote_copy(
            src_ref=(to_right if side == "right" else to_left).at[rows, :],
            dst_ref=(left_half if side == "right" else right_half).at[rows, :],
            send_sem=range_send.at[direction, 1, step],
            recv_sem=range_recv.at[direction, 1, step],
            device_id=to[side], device_id_type=MESH,
        )

    def relayed(side, step):
        return jnp.logical_and(source[side], step >= chunks - source_count[side])

    def to_relay(side, step, piece):
        rows = pl.ds(pl.multiple_of(chunk_at(step, chunks) * CHUNK, CHUNK), CHUNK)
        direction = 0 if side == "right" else 1
        cols = pl.ds(cells - HALF, HALF) if side == "right" else pl.ds(0, HALF)
        device = (az, jnp.minimum(rg + width, rg_count - 1) if side == "right" else jnp.maximum(rg - width, 0))
        if piece == 0:
            return pltpu.make_async_remote_copy(
                src_ref=raw.at[:, rows, cols], dst_ref=relay.at[:, rows, :],
                send_sem=range_send.at[direction, 0, step], recv_sem=relay_recv.at[0, step],
                device_id=device, device_id_type=MESH,
            )
        return pltpu.make_async_remote_copy(
            src_ref=(to_right if side == "right" else to_left).at[rows, :], dst_ref=relay_half.at[rows, :],
            send_sem=range_send.at[direction, 1, step], recv_sem=relay_recv.at[1, step],
            device_id=device, device_id_type=MESH,
        )

    def from_relay(side, step, piece):
        rows = pl.ds(pl.multiple_of(chunk_at(step, chunks) * CHUNK, CHUNK), CHUNK)
        direction = 0 if side == "right" else 1
        device = (az, jnp.maximum(rg - width + 1, 0) if side == "right" else jnp.minimum(rg + width - 1, rg_count - 1))
        if piece == 0:
            return pltpu.make_async_remote_copy(
                src_ref=relay.at[:, rows, :], dst_ref=(left if side == "right" else right).at[:, rows, :],
                send_sem=relay_send.at[0, step], recv_sem=range_recv.at[direction, 0, step],
                device_id=device, device_id_type=MESH,
            )
        return pltpu.make_async_remote_copy(
            src_ref=relay_half.at[rows, :], dst_ref=(left_half if side == "right" else right_half).at[rows, :],
            send_sem=relay_send.at[1, step], recv_sem=range_recv.at[direction, 1, step],
            device_id=device, device_id_type=MESH,
        )

    def send_wide(side, step):
        @pl.when(jnp.logical_and(there[side], jnp.logical_not(relayed(side, step))))
        def _():
            wide_copy(side, step).start()

        @pl.when(relayed(side, step))
        def _():
            to_relay(side, step, 0).start()

    def send_half(side, step):
        @pl.when(jnp.logical_and(there[side], jnp.logical_not(relayed(side, step))))
        def _():
            half_copy(side, step).start()

        @pl.when(relayed(side, step))
        def _():
            to_relay(side, step, 1).start()

    for side in ("right", "left"):
        send_wide(side, 0)

    load.wait()
    low = lax.broadcasted_iota(jnp.int32, (CHUNK, BLK), 1) < BLK // 2

    @pl.loop(0, chunks)
    def _(c):
        rows = pl.ds(pl.multiple_of(c * CHUNK, CHUNK), CHUNK)
        real, imag = own[0, rows, 0:BLK].astype(F32), own[1, rows, 0:BLK].astype(F32)
        to_right[rows, :] = jnp.where(low, pltpu.roll(real, BLK // 2, 1), imag).astype(BF16)
        real = own[0, rows, cells - BLK : cells].astype(F32)
        imag = own[1, rows, cells - BLK : cells].astype(F32)
        to_left[rows, :] = jnp.where(low, real, pltpu.roll(imag, BLK // 2, 1)).astype(BF16)

    @pl.loop(0, chunks)
    def _(step):
        for side in ("right", "left"):
            @pl.when(step > 0)
            def _(side=side):
                send_wide(side, step)
            send_half(side, step)

    @pl.when(jnp.logical_not(has_left))
    def _():
        left[...] = jnp.zeros_like(left)
        left_half[...] = jnp.zeros_like(left_half)

    @pl.when(jnp.logical_not(has_right))
    def _():
        right[...] = jnp.zeros_like(right)
        right_half[...] = jnp.zeros_like(right_half)

    @pl.when(jnp.logical_not(has_before))
    def _():
        migrated[0:HALF, :] = jnp.zeros((HALF, 2 * cells), BF16)

    @pl.when(jnp.logical_not(has_after))
    def _():
        migrated[HALF + lines :, :] = jnp.zeros((HALF, 2 * cells), BF16)

    total[...] = jnp.zeros_like(total)

    for copy in small:
        copy.wait()

    tap_count = taps.shape[0]
    row = lax.broadcasted_iota(jnp.int32, (2 * BLK, BLK), 0)
    column = lax.broadcasted_iota(jnp.int32, (2 * BLK, BLK), 1)
    toep[...] = jnp.zeros_like(toep)
    for part in range(2):
        rolled = toeplitz_tiles(chirp[part : part + 1, :].astype(F32), False)
        for d in range(5):
            tile = rolled[:, d * BLK : (d + 1) * BLK].T.astype(BF16)
            for p in range(2):
                u = d + p
                toep[part * 6 * BLK + u * BLK : part * 6 * BLK + (u + 1) * BLK, p * BLK : (p + 1) * BLK] = tile
    for b in range(blocks):
        offset = row - column - (shift[b] + MAXS)
        cell = rg * cells + b * BLK - BLK // 2 + row
        inside = jnp.logical_and(cell >= 0, cell < rg_count * cells)
        matrix = jnp.zeros((2 * BLK, BLK), F32)
        for k in range(tap_count):
            weight = jnp.broadcast_to(taps[k : k + 1, b * BLK : (b + 1) * BLK].astype(F32), matrix.shape)
            matrix = matrix + jnp.where(offset == k, weight, 0.0)
        matrix = jnp.where(inside, matrix, 0.0).astype(BF16)
        both = jnp.dot(toep[...], matrix, preferred_element_type=F32)
        real, imag = both[: 6 * BLK], both[6 * BLK :]
        filters[0] = jnp.concatenate([real, -imag], axis=1).astype(BF16)
        filters[1] = jnp.concatenate([imag, real], axis=1).astype(BF16)
        at = 0
        if b == 0:
            pieces = [(0, 64, 320), (1, 64, 320), (0, 320, 704), (1, 320, 704),
                      (0, 704, 768), None, (1, 704, 768), None, (0, 0, 64), (1, 0, 64)]
        elif b == 1:
            pieces = [None, (0, 0, 192), None, (1, 0, 192), (0, 192, 576), (1, 192, 576),
                      (0, 576, 768), None, (1, 576, 768), None]
        else:
            pieces = [None, (0, 0, 64), None, (1, 0, 64), (0, 64, 448), (1, 64, 448),
                      (0, 448, 704), (1, 448, 704), (0, 704, 768), (1, 704, 768)]
        for piece in pieces:
            if piece is None:
                weights[b, at : at + 64, :] = jnp.zeros((64, 2 * BLK), BF16)
                at += 64
            else:
                part, start, stop = piece
                weights[b, at : at + stop - start, :] = filters[part, start:stop, :]
                at += stop - start

    for b in range(blocks):
        for part in range(2):
            rolled = toeplitz_tiles(azimuth[b, part : part + 1, :].astype(F32), True).astype(BF16)
            for q in range(5):
                lane = (8 - q) % 8 * BLK
                azimuth_rows[b, q * BLK : (q + 1) * BLK, part * BLK : (part + 1) * BLK] = rolled[:, lane : lane + BLK]

    def turned(tile):
        real, imag = tile[:, :BLK], tile[:, BLK:]
        return jnp.concatenate([tile, jnp.concatenate([imag, -real], axis=1)], axis=0)

    def add_lines(source, first, count, target):
        for b in range(blocks):
            tile = turned(migrated[source, 2 * b * BLK : 2 * (b + 1) * BLK])
            result = jnp.dot(azimuth_rows[b, first : first + count, :], tile, preferred_element_type=F32)
            columns = slice(b * BLK, (b + 1) * BLK)
            total[0, target, columns] += result[:, :BLK]
            total[1, target, columns] += result[:, BLK:]

    def line_source(step, half):
        start = HALF + chunk_of(step, chunks) * CHUNK + half * (CHUNK // 2)
        return migrated.at[pl.ds(pl.multiple_of(start, CHUNK // 2), CHUNK // 2), :]

    def line_target(step, half):
        start = jnp.where(step % 2 == 0, HALF + lines + step // 2 * CHUNK, CHUNK - step // 2 * CHUNK)
        return migrated.at[pl.ds(pl.multiple_of(start + half * (CHUNK // 2), CHUNK // 2), CHUNK // 2), :]

    def is_passed(step, half):
        found = jnp.bool_(False)
        for at_step, at_half, sender, _, target in passed:
            if at_half == half and target == middle:
                found = jnp.logical_or(found, jnp.logical_and(az == sender, step == at_step))
        return found

    def line_to_relay(entry):
        step, half, _, via, _ = entry
        return pltpu.make_async_remote_copy(
            src_ref=line_source(step, half), dst_ref=relay_lines,
            send_sem=azimuth_send.at[step, half], recv_sem=lines_recv,
            device_id=(via, rg), device_id_type=MESH,
        )

    def line_from_relay(entry):
        step, half, _, _, target = entry
        return pltpu.make_async_remote_copy(
            src_ref=relay_lines, dst_ref=line_target(step, half),
            send_sem=lines_send, recv_sem=azimuth_recv.at[step, half],
            device_id=(target, rg), device_id_type=MESH,
        )

    def line_copy(step, half):
        device = (jnp.where(step % 2 == 0, to["before"][0], to["after"][0]), rg)
        return pltpu.make_async_remote_copy(
            src_ref=line_source(step, half), dst_ref=line_target(step, half),
            send_sem=azimuth_send.at[step, half], recv_sem=azimuth_recv.at[step, half],
            device_id=device, device_id_type=MESH,
        )

    @pl.loop(0, chunks)
    def _(step):
        c = chunk_at(step, chunks)
        rows = pl.ds(pl.multiple_of(c * CHUNK, CHUNK), CHUNK)

        @pl.when(step == chunks - 1)
        def _():
            for s in range(4):
                @pl.when(has_after if s % 2 == 0 else has_before)
                def _(s=s):
                    for half in range(2):
                        line_copy(s, half).wait_recv()
            add_lines(slice(0, 128), 512, 128, slice(256, 384))
            add_lines(slice(128, 256), 384, 256, slice(256, 512))
            add_lines(slice(HALF + lines, HALF + lines + 128), 0, 256, slice(lines, lines + 256))
            add_lines(slice(HALF + lines + 128, HALF + lines + 256), 0, 128, slice(lines + 128, lines + 256))

        for entry in passed:
            @pl.when(jnp.logical_and(az == entry[3], step == (6 if entry[3] == middle + 1 else {1: 1, 3: 2}.get(entry[0], 3))))
            def _(entry=entry):
                line_to_relay(entry).wait_recv()
                line_from_relay(entry).start()

        for side, exists in (("right", has_left), ("left", has_right)):
            @pl.when(exists)
            def _(side=side):
                wide_copy(side, step).wait_recv()
                half_copy(side, step).wait_recv()

        own_parts = [own[0, rows, :], own[1, rows, :]]
        for b in range(blocks):
            if b == 0:
                parts = [left[0, rows, :], left[1, rows, :]] + own_parts + [
                    right[0, rows, :BLK], right[1, rows, :BLK], left_half[rows, :]]
            elif b == 1:
                parts = [left[0, rows, :], left[1, rows, :]] + own_parts + [right[0, rows, :], right[1, rows, :]]
            else:
                parts = [left[0, rows, BLK:], left[1, rows, BLK:]] + own_parts + [
                    right[0, rows, :], right[1, rows, :], right_half[rows, :]]
            joined = jnp.concatenate(parts, axis=1)
            depth = joined.shape[1]
            result = jnp.dot(joined, weights[b, :depth, :], preferred_element_type=F32)
            migrated[pl.ds(pl.multiple_of(HALF + c * CHUNK, CHUNK), CHUNK), 2 * b * BLK : 2 * (b + 1) * BLK] = result.astype(BF16)

        @pl.when(step < 4)
        def _():
            place = place_at(step)
            exists = jnp.where(place % 2 == 0, jnp.logical_and(has_before, jnp.logical_not(opens)), has_after)
            for half in range(2):
                @pl.when(jnp.logical_and(exists, jnp.logical_not(is_passed(place, half))))
                def _(half=half):
                    line_copy(place, half).start()
            for entry in passed:
                if entry[4] == middle:
                    @pl.when(jnp.logical_and(az == entry[2], place == entry[0]))
                    def _(entry=entry):
                        line_to_relay(entry).start()

        @pl.when(jnp.logical_and(opens, step == 4))
        def _():
            pl.semaphore_wait(ready, len(answering))
            through = {(entry[0], entry[1]): entry for entry in passed if entry[2] == middle}
            for s in (0, 2):
                for half in range(2):
                    if (s, half) in through:
                        line_to_relay(through[s, half]).start()
                    else:
                        line_copy(s, half).start()

        for side in ("left", "right"):
            for late in (chunks - 2 * (heights - 1), step + AHEAD):
                first = isinstance(late, int)
                @pl.when(jnp.logical_and(
                    jnp.logical_and(relaying[side], late >= chunks - relay_count[side]),
                    step == 0 if first else late < chunks,
                ))
                def _(side=side, late=late):
                    for piece in range(2):
                        to_relay(side, late, piece).wait_recv()
                        from_relay(side, late, piece).start()

        @pl.when(step < chunks - 1)
        def _():
            add_lines(pl.ds(pl.multiple_of(HALF + c * CHUNK, CHUNK), CHUNK), 0, 5 * BLK,
                      pl.ds(pl.multiple_of(c * CHUNK, CHUNK), 5 * BLK))

    @pl.loop(0, chunks)
    def _(step):
        for side in ("right", "left"):
            @pl.when(there[side])
            def _(side=side):
                wide_copy(side, step).wait_send()
                half_copy(side, step).wait_send()

    for s in range(4):
        @pl.when(has_before if s % 2 == 0 else has_after)
        def _(s=s):
            for half in range(2):
                line_copy(s, half).wait_send()

    @pl.loop(0, chunks)
    def _(step):
        for side in ("left", "right"):
            @pl.when(jnp.logical_and(relaying[side], step >= chunks - relay_count[side]))
            def _(side=side):
                for piece in range(2):
                    from_relay(side, step, piece).wait_send()

    for entry in passed:
        @pl.when(az == entry[3])
        def _(entry=entry):
            line_from_relay(entry).wait_send()


def finish(total, lines_in, azimuth_rows, out, stage, sems):
    lines, blocks = out.shape[1], azimuth_rows.shape[0]
    last = lines // 2
    start, stop = last - HALF, last + CHUNK + HALF
    copies = [
        pltpu.make_async_copy(total.at[:, HALF : HALF + start, :], out.at[:, 0:start, :], sems.at[0]),
        pltpu.make_async_copy(total.at[:, HALF + stop : HALF + lines, :], out.at[:, stop:lines, :], sems.at[1]),
    ]
    for copy in copies:
        copy.start()
    tiles = []
    for b in range(blocks):
        tile = lines_in[HALF + last : HALF + last + CHUNK, 2 * b * BLK : 2 * (b + 1) * BLK]
        real, imag = tile[:, :BLK], tile[:, BLK:]
        tiles.append(jnp.concatenate([tile, jnp.concatenate([imag, -real], axis=1)], axis=0))
    at = 0
    for piece, rows in enumerate((256, 256, 128)):
        for b in range(blocks):
            result = jnp.dot(azimuth_rows[b, at : at + rows, :], tiles[b], preferred_element_type=F32)
            columns = slice(b * BLK, (b + 1) * BLK)
            source = slice(HALF + start + at, HALF + start + at + rows)
            stage[0, at : at + rows, columns] = total[0, source, columns] + result[:, :BLK]
            stage[1, at : at + rows, columns] = total[1, source, columns] + result[:, BLK:]
        copy = pltpu.make_async_copy(
            stage.at[:, at : at + rows, :], out.at[:, start + at : start + at + rows, :], sems.at[2 + piece]
        )
        copy.start()
        copies.append(copy)
        at += rows
    for copy in copies:
        copy.wait()


def per_device(ranks, raw_echo, range_chirp, migration_taps, block_shift, azimuth_chirp):
    lines, cells = raw_echo.shape[1:]
    blocks = cells // BLK
    chunks = lines // CHUNK
    vmem = pl.BlockSpec(memory_space=pltpu.VMEM)
    hbm = pl.BlockSpec(memory_space=pltpu.HBM)
    total, migrated, azimuth_rows = pl.pallas_call(
        functools.partial(kernel, ranks),
        out_shape=(
            pltpu.VMEM((2, lines + 2 * HALF, cells), F32),
            pltpu.VMEM((lines + 2 * HALF, 2 * cells), BF16),
            pltpu.VMEM((blocks, 5 * BLK, 2 * BLK), BF16),
        ),
        in_specs=[hbm] * 5,
        out_specs=(vmem, vmem, vmem),
        scratch_shapes=[
            pltpu.VMEM((2, lines, cells), BF16),
            pltpu.VMEM((2, lines, HALF), BF16),
            pltpu.VMEM((2, lines, HALF), BF16),
            pltpu.VMEM((lines, BLK), BF16),
            pltpu.VMEM((lines, BLK), BF16),
            pltpu.VMEM((lines, BLK), BF16),
            pltpu.VMEM((lines, BLK), BF16),
            pltpu.VMEM((2, lines, HALF), BF16),
            pltpu.VMEM((lines, BLK), BF16),
            pltpu.VMEM((CHUNK // 2, 2 * cells), BF16),
            pltpu.VMEM((2, 6 * BLK, 2 * BLK), BF16),
            pltpu.VMEM((12 * BLK, 2 * BLK), BF16),
            pltpu.VMEM((blocks, 14 * BLK, 2 * BLK), BF16),
            pltpu.VMEM(range_chirp.shape, BF16),
            pltpu.VMEM(migration_taps.shape, BF16),
            pltpu.SMEM(block_shift.shape, jnp.int32),
            pltpu.VMEM(azimuth_chirp.shape, BF16),
            pltpu.SemaphoreType.DMA,
            pltpu.SemaphoreType.DMA((4,)),
            pltpu.SemaphoreType.DMA((2, 2, chunks)),
            pltpu.SemaphoreType.DMA((2, 2, chunks)),
            pltpu.SemaphoreType.DMA((4, 2)),
            pltpu.SemaphoreType.DMA((4, 2)),
            pltpu.SemaphoreType.DMA((2, chunks)),
            pltpu.SemaphoreType.DMA((2, chunks)),
            pltpu.SemaphoreType.DMA,
            pltpu.SemaphoreType.DMA,
            pltpu.SemaphoreType.REGULAR,
        ],
        compiler_params=pltpu.CompilerParams(collective_id=0, has_side_effects=True, vmem_limit_bytes=40 << 20),
        name="focus",
    )(*(
        pltpu.with_memory_space_constraint(value, pltpu.HBM)
        for value in (raw_echo, range_chirp, migration_taps, block_shift, azimuth_chirp)
    ))
    return pl.pallas_call(
        finish,
        out_shape=jax.ShapeDtypeStruct((2, lines, cells), F32),
        in_specs=[vmem, vmem, vmem],
        out_specs=hbm,
        scratch_shapes=[
            pltpu.VMEM((2, 2 * HALF + CHUNK, cells), F32),
            pltpu.SemaphoreType.DMA((5,)),
        ],
        compiler_params=pltpu.CompilerParams(vmem_limit_bytes=40 << 20),
        name="finish",
    )(total, migrated, azimuth_rows)


def solution(mesh):
    ranks = (mesh.shape["az"], mesh.shape["rg"])
    placed = (P(None, "az", "rg"), P(), P(None, "rg"), P("rg"), P("rg", None, None))
    return jax.shard_map(
        functools.partial(per_device, ranks), mesh=mesh, in_specs=placed, out_specs=P(None, "az", "rg"), check_vma=False
    )
```

```python
import functools

import jax
import jax.numpy as jnp
from jax import lax
from jax.experimental import pallas as pl
from jax.experimental.pallas import tpu as pltpu
from jax.sharding import PartitionSpec as P

MESH = pl.DeviceIdType.MESH
BLK = 128
HALF = 256
MAXS = 60
CHUNK = 128
AHEAD = 3
BF16 = jnp.bfloat16
F32 = jnp.float32


def chunk_of(place, chunks):
    return jnp.where(place % 2 == 0, place // 2, chunks - 1 - place // 2)


def toeplitz_tiles(taps_row, front):
    zeros = jnp.zeros_like(taps_row)
    parts = [zeros, taps_row] if front else [taps_row, zeros]
    base = jnp.broadcast_to(jnp.concatenate(parts, axis=1), (BLK, 2 * taps_row.shape[1]))
    return pltpu.roll(base, 0, 1, stride=1, stride_axis=0)


def kernel(
    ranks, raw, chirp_in, taps_in, shift_in, azimuth_in, total, migrated, azimuth_rows,
    own, left, right, left_half, right_half, to_right, to_left, relay, relay_half, relay_lines,
    filters, toep, weights, chirp, taps, shift, azimuth,
    own_sem, small_sem, range_send, range_recv, azimuth_send, azimuth_recv,
    relay_send, relay_recv, lines_send, lines_recv, ready,
):
    az_count, rg_count = ranks
    az, rg = lax.axis_index("az"), lax.axis_index("rg")
    lines, cells = own.shape[1], own.shape[2]
    blocks = cells // BLK
    chunks = lines // CHUNK
    has_left, has_right = rg > 0, rg < rg_count - 1
    has_before, has_after = az > 0, az < az_count - 1
    to = {
        "left": (az, jnp.maximum(rg - 1, 0)),
        "right": (az, jnp.minimum(rg + 1, rg_count - 1)),
        "before": (jnp.maximum(az - 1, 0), rg),
        "after": (jnp.minimum(az + 1, az_count - 1), rg),
    }
    there = {"left": has_left, "right": has_right, "before": has_before, "after": has_after}
    width = 4 if rg_count >= 8 else 2
    heights = rg_count // width
    y, column_at = rg // width, rg % width
    first_column, last_column = column_at == 0, column_at == width - 1
    up, down = y > 0, y < heights - 1
    source = {"left": jnp.logical_and(first_column, up), "right": jnp.logical_and(last_column, down)}
    relaying = {"left": jnp.logical_and(first_column, down), "right": jnp.logical_and(last_column, up)}
    source_count = {"left": 2 * (heights - y), "right": 2 * (y + 1)}
    relay_count = {"left": 2 * (heights - y - 1), "right": 2 * y}
    middle = az_count // 2
    passed = [] if az_count < 12 else [
        (1, 0, middle - 1, az_count - 2, middle),
        (1, 1, middle - 1, az_count - 3, middle),
        (3, 1, middle - 1, az_count - 4, middle),
        (3, 0, middle - 1, middle + 1, middle),
        (0, 0, middle, middle - 2, middle - 1),
        (0, 1, middle, middle - 3, middle - 1),
        (2, 1, middle, middle - 4, middle - 1),
    ]
    opens, answers = az == middle, az == middle - 1
    both = [
        (to["left"], has_left), (to["right"], has_right),
        ((az, jnp.maximum(rg - width, 0)), source["left"]),
        ((az, jnp.minimum(rg + width, rg_count - 1)), relaying["left"]),
        ((az, jnp.minimum(rg + width - 1, rg_count - 1)), relaying["left"]),
        ((az, jnp.maximum(rg - width + 1, 0)), source["right"]),
        ((az, jnp.minimum(rg + width, rg_count - 1)), source["right"]),
        ((az, jnp.maximum(rg - width, 0)), relaying["right"]),
        ((az, jnp.maximum(rg - width + 1, 0)), relaying["right"]),
        ((az, jnp.minimum(rg + width - 1, rg_count - 1)), source["left"]),
    ]
    greet = both + [
        (to["before"], has_before), (to["after"], jnp.logical_and(has_after, jnp.logical_not(answers))),
    ]
    expect = [exists for _, exists in both] + [jnp.logical_and(has_before, jnp.logical_not(opens)), has_after]
    answering = [answers]
    for _, _, sender, via, target in passed:
        greet.append(((via, rg), opens))
        expect.append(az == via)
        if target == middle:
            greet.append(((sender, rg), az == via))
            expect.append(az == sender)
        else:
            greet.append(((via, rg), az == target))
            expect.append(az == via)
            answering.append(az == via)

    def place_at(step):
        early = jnp.where(step < 2, 2 * step + 1, 2 * step - 4)
        return jnp.where(jnp.logical_and(answers, step < 4), early, step)

    def chunk_at(step, chunks):
        return chunk_of(place_at(step), chunks)

    load = pltpu.make_async_copy(raw, own, own_sem)
    load.start()
    small = [
        pltpu.make_async_copy(source, place, small_sem.at[i])
        for i, (source, place) in enumerate(
            ((chirp_in, chirp), (taps_in, taps), (shift_in, shift), (azimuth_in, azimuth))
        )
    ]
    for copy in small:
        copy.start()

    barrier = pltpu.get_barrier_semaphore()
    count = 0
    for device, exists in greet:
        @pl.when(exists)
        def _(device=device):
            pl.semaphore_signal(barrier, inc=1, device_id=device, device_id_type=MESH)
    for exists in expect:
        count = count + jnp.where(exists, 1, 0)
    pl.semaphore_wait(barrier, count)
    for exists in answering:
        @pl.when(exists)
        def _():
            pl.semaphore_signal(ready, inc=1, device_id=(middle, rg), device_id_type=MESH)

    def wide_copy(side, step):
        rows = pl.ds(pl.multiple_of(chunk_at(step, chunks) * CHUNK, CHUNK), CHUNK)
        direction = 0 if side == "right" else 1
        cols = pl.ds(cells - HALF, HALF) if side == "right" else pl.ds(0, HALF)
        return pltpu.make_async_remote_copy(
            src_ref=raw.at[:, rows, cols],
            dst_ref=(left if side == "right" else right).at[:, rows, :],
            send_sem=range_send.at[direction, 0, step],
            recv_sem=range_recv.at[direction, 0, step],
            device_id=to[side], device_id_type=MESH,
        )

    def half_copy(side, step):
        rows = pl.ds(pl.multiple_of(chunk_at(step, chunks) * CHUNK, CHUNK), CHUNK)
        direction = 0 if side == "right" else 1
        return pltpu.make_async_remote_copy(
            src_ref=(to_right if side == "right" else to_left).at[rows, :],
            dst_ref=(left_half if side == "right" else right_half).at[rows, :],
            send_sem=range_send.at[direction, 1, step],
            recv_sem=range_recv.at[direction, 1, step],
            device_id=to[side], device_id_type=MESH,
        )

    def relayed(side, step):
        return jnp.logical_and(source[side], step >= chunks - source_count[side])

    def to_relay(side, step, piece):
        rows = pl.ds(pl.multiple_of(chunk_at(step, chunks) * CHUNK, CHUNK), CHUNK)
        direction = 0 if side == "right" else 1
        cols = pl.ds(cells - HALF, HALF) if side == "right" else pl.ds(0, HALF)
        device = (az, jnp.minimum(rg + width, rg_count - 1) if side == "right" else jnp.maximum(rg - width, 0))
        if piece == 0:
            return pltpu.make_async_remote_copy(
                src_ref=raw.at[:, rows, cols], dst_ref=relay.at[:, rows, :],
                send_sem=range_send.at[direction, 0, step], recv_sem=relay_recv.at[0, step],
                device_id=device, device_id_type=MESH,
            )
        return pltpu.make_async_remote_copy(
            src_ref=(to_right if side == "right" else to_left).at[rows, :], dst_ref=relay_half.at[rows, :],
            send_sem=range_send.at[direction, 1, step], recv_sem=relay_recv.at[1, step],
            device_id=device, device_id_type=MESH,
        )

    def from_relay(side, step, piece):
        rows = pl.ds(pl.multiple_of(chunk_at(step, chunks) * CHUNK, CHUNK), CHUNK)
        direction = 0 if side == "right" else 1
        device = (az, jnp.maximum(rg - width + 1, 0) if side == "right" else jnp.minimum(rg + width - 1, rg_count - 1))
        if piece == 0:
            return pltpu.make_async_remote_copy(
                src_ref=relay.at[:, rows, :], dst_ref=(left if side == "right" else right).at[:, rows, :],
                send_sem=relay_send.at[0, step], recv_sem=range_recv.at[direction, 0, step],
                device_id=device, device_id_type=MESH,
            )
        return pltpu.make_async_remote_copy(
            src_ref=relay_half.at[rows, :], dst_ref=(left_half if side == "right" else right_half).at[rows, :],
            send_sem=relay_send.at[1, step], recv_sem=range_recv.at[direction, 1, step],
            device_id=device, device_id_type=MESH,
        )

    def send_wide(side, step):
        @pl.when(jnp.logical_and(there[side], jnp.logical_not(relayed(side, step))))
        def _():
            wide_copy(side, step).start()

        @pl.when(relayed(side, step))
        def _():
            to_relay(side, step, 0).start()

    def send_half(side, step):
        @pl.when(jnp.logical_and(there[side], jnp.logical_not(relayed(side, step))))
        def _():
            half_copy(side, step).start()

        @pl.when(relayed(side, step))
        def _():
            to_relay(side, step, 1).start()

    for side in ("right", "left"):
        send_wide(side, 0)

    load.wait()
    low = lax.broadcasted_iota(jnp.int32, (CHUNK, BLK), 1) < BLK // 2

    @pl.loop(0, chunks)
    def _(c):
        rows = pl.ds(pl.multiple_of(c * CHUNK, CHUNK), CHUNK)
        real, imag = own[0, rows, 0:BLK].astype(F32), own[1, rows, 0:BLK].astype(F32)
        to_right[rows, :] = jnp.where(low, pltpu.roll(real, BLK // 2, 1), imag).astype(BF16)
        real = own[0, rows, cells - BLK : cells].astype(F32)
        imag = own[1, rows, cells - BLK : cells].astype(F32)
        to_left[rows, :] = jnp.where(low, real, pltpu.roll(imag, BLK // 2, 1)).astype(BF16)

    @pl.loop(0, chunks)
    def _(step):
        for side in ("right", "left"):
            @pl.when(step > 0)
            def _(side=side):
                send_wide(side, step)
            send_half(side, step)

    @pl.when(jnp.logical_not(has_left))
    def _():
        left[...] = jnp.zeros_like(left)
        left_half[...] = jnp.zeros_like(left_half)

    @pl.when(jnp.logical_not(has_right))
    def _():
        right[...] = jnp.zeros_like(right)
        right_half[...] = jnp.zeros_like(right_half)

    @pl.when(jnp.logical_not(has_before))
    def _():
        migrated[0:HALF, :] = jnp.zeros((HALF, 2 * cells), BF16)

    @pl.when(jnp.logical_not(has_after))
    def _():
        migrated[HALF + lines :, :] = jnp.zeros((HALF, 2 * cells), BF16)

    total[...] = jnp.zeros_like(total)

    for copy in small:
        copy.wait()

    tap_count = taps.shape[0]
    row = lax.broadcasted_iota(jnp.int32, (2 * BLK, BLK), 0)
    column = lax.broadcasted_iota(jnp.int32, (2 * BLK, BLK), 1)
    toep[...] = jnp.zeros_like(toep)
    for part in range(2):
        rolled = toeplitz_tiles(chirp[part : part + 1, :].astype(F32), False)
        for d in range(5):
            tile = rolled[:, d * BLK : (d + 1) * BLK].T.astype(BF16)
            for p in range(2):
                u = d + p
                toep[part * 6 * BLK + u * BLK : part * 6 * BLK + (u + 1) * BLK, p * BLK : (p + 1) * BLK] = tile
    for b in range(blocks):
        offset = row - column - (shift[b] + MAXS)
        cell = rg * cells + b * BLK - BLK // 2 + row
        inside = jnp.logical_and(cell >= 0, cell < rg_count * cells)
        matrix = jnp.zeros((2 * BLK, BLK), F32)
        for k in range(tap_count):
            weight = jnp.broadcast_to(taps[k : k + 1, b * BLK : (b + 1) * BLK].astype(F32), matrix.shape)
            matrix = matrix + jnp.where(offset == k, weight, 0.0)
        matrix = jnp.where(inside, matrix, 0.0).astype(BF16)
        both = jnp.dot(toep[...], matrix, preferred_element_type=F32)
        real, imag = both[: 6 * BLK], both[6 * BLK :]
        filters[0] = jnp.concatenate([real, -imag], axis=1).astype(BF16)
        filters[1] = jnp.concatenate([imag, real], axis=1).astype(BF16)
        at = 0
        if b == 0:
            pieces = [(0, 64, 320), (1, 64, 320), (0, 320, 704), (1, 320, 704),
                      (0, 704, 768), None, (1, 704, 768), None, (0, 0, 64), (1, 0, 64)]
        elif b == 1:
            pieces = [None, (0, 0, 192), None, (1, 0, 192), (0, 192, 576), (1, 192, 576),
                      (0, 576, 768), None, (1, 576, 768), None]
        else:
            pieces = [None, (0, 0, 64), None, (1, 0, 64), (0, 64, 448), (1, 64, 448),
                      (0, 448, 704), (1, 448, 704), (0, 704, 768), (1, 704, 768)]
        for piece in pieces:
            if piece is None:
                weights[b, at : at + 64, :] = jnp.zeros((64, 2 * BLK), BF16)
                at += 64
            else:
                part, start, stop = piece
                weights[b, at : at + stop - start, :] = filters[part, start:stop, :]
                at += stop - start

    for b in range(blocks):
        for part in range(2):
            rolled = toeplitz_tiles(azimuth[b, part : part + 1, :].astype(F32), True).astype(BF16)
            for q in range(5):
                lane = (8 - q) % 8 * BLK
                azimuth_rows[b, q * BLK : (q + 1) * BLK, part * BLK : (part + 1) * BLK] = rolled[:, lane : lane + BLK]

    def turned(tile):
        real, imag = tile[:, :BLK], tile[:, BLK:]
        return jnp.concatenate([tile, jnp.concatenate([imag, -real], axis=1)], axis=0)

    def add_lines(source, first, count, target):
        for b in range(blocks):
            tile = turned(migrated[source, 2 * b * BLK : 2 * (b + 1) * BLK])
            result = jnp.dot(azimuth_rows[b, first : first + count, :], tile, preferred_element_type=F32)
            columns = slice(b * BLK, (b + 1) * BLK)
            total[0, target, columns] += result[:, :BLK]
            total[1, target, columns] += result[:, BLK:]

    def line_source(step, half):
        start = HALF + chunk_of(step, chunks) * CHUNK + half * (CHUNK // 2)
        return migrated.at[pl.ds(pl.multiple_of(start, CHUNK // 2), CHUNK // 2), :]

    def line_target(step, half):
        start = jnp.where(step % 2 == 0, HALF + lines + step // 2 * CHUNK, CHUNK - step // 2 * CHUNK)
        return migrated.at[pl.ds(pl.multiple_of(start + half * (CHUNK // 2), CHUNK // 2), CHUNK // 2), :]

    def is_passed(step, half):
        found = jnp.bool_(False)
        for at_step, at_half, sender, _, target in passed:
            if at_half == half and target == middle:
                found = jnp.logical_or(found, jnp.logical_and(az == sender, step == at_step))
        return found

    def line_to_relay(entry):
        step, half, _, via, _ = entry
        return pltpu.make_async_remote_copy(
            src_ref=line_source(step, half), dst_ref=relay_lines,
            send_sem=azimuth_send.at[step, half], recv_sem=lines_recv,
            device_id=(via, rg), device_id_type=MESH,
        )

    def line_from_relay(entry):
        step, half, _, _, target = entry
        return pltpu.make_async_remote_copy(
            src_ref=relay_lines, dst_ref=line_target(step, half),
            send_sem=lines_send, recv_sem=azimuth_recv.at[step, half],
            device_id=(target, rg), device_id_type=MESH,
        )

    def line_copy(step, half):
        device = (jnp.where(step % 2 == 0, to["before"][0], to["after"][0]), rg)
        return pltpu.make_async_remote_copy(
            src_ref=line_source(step, half), dst_ref=line_target(step, half),
            send_sem=azimuth_send.at[step, half], recv_sem=azimuth_recv.at[step, half],
            device_id=device, device_id_type=MESH,
        )

    def sent(first, last):
        @pl.loop(first, last)
        def _(step):
            for side in ("right", "left"):
                @pl.when(there[side])
                def _(side=side):
                    wide_copy(side, step).wait_send()
                    half_copy(side, step).wait_send()

    @pl.loop(0, chunks)
    def _(step):
        c = chunk_at(step, chunks)
        rows = pl.ds(pl.multiple_of(c * CHUNK, CHUNK), CHUNK)

        @pl.when(step == chunks - 1)
        def _():
            for s in range(4):
                @pl.when(has_after if s % 2 == 0 else has_before)
                def _(s=s):
                    for half in range(2):
                        line_copy(s, half).wait_recv()
            add_lines(slice(0, 128), 512, 128, slice(256, 384))
            add_lines(slice(128, 256), 384, 256, slice(256, 512))
            add_lines(slice(HALF + lines, HALF + lines + 128), 0, 256, slice(lines, lines + 256))
            add_lines(slice(HALF + lines + 128, HALF + lines + 256), 0, 128, slice(lines + 128, lines + 256))
            sent(0, chunks - 2)

        for entry in passed:
            @pl.when(jnp.logical_and(az == entry[3], step == (6 if entry[3] == middle + 1 else {1: 1, 3: 2, 2: 4}.get(entry[0], 3))))
            def _(entry=entry):
                line_to_relay(entry).wait_recv()
                line_from_relay(entry).start()

        for side, exists in (("right", has_left), ("left", has_right)):
            @pl.when(exists)
            def _(side=side):
                wide_copy(side, step).wait_recv()
                half_copy(side, step).wait_recv()

        own_parts = [own[0, rows, :], own[1, rows, :]]
        for b in range(blocks):
            if b == 0:
                parts = [left[0, rows, :], left[1, rows, :]] + own_parts + [
                    right[0, rows, :BLK], right[1, rows, :BLK], left_half[rows, :]]
            elif b == 1:
                parts = [left[0, rows, :], left[1, rows, :]] + own_parts + [right[0, rows, :], right[1, rows, :]]
            else:
                parts = [left[0, rows, BLK:], left[1, rows, BLK:]] + own_parts + [
                    right[0, rows, :], right[1, rows, :], right_half[rows, :]]
            joined = jnp.concatenate(parts, axis=1)
            depth = joined.shape[1]
            result = jnp.dot(joined, weights[b, :depth, :], preferred_element_type=F32)
            migrated[pl.ds(pl.multiple_of(HALF + c * CHUNK, CHUNK), CHUNK), 2 * b * BLK : 2 * (b + 1) * BLK] = result.astype(BF16)

        @pl.when(step < 4)
        def _():
            place = place_at(step)
            exists = jnp.where(place % 2 == 0, jnp.logical_and(has_before, jnp.logical_not(opens)), has_after)
            for half in range(2):
                @pl.when(jnp.logical_and(exists, jnp.logical_not(is_passed(place, half))))
                def _(half=half):
                    line_copy(place, half).start()
            for entry in passed:
                if entry[4] == middle:
                    @pl.when(jnp.logical_and(az == entry[2], place == entry[0]))
                    def _(entry=entry):
                        line_to_relay(entry).start()

        @pl.when(jnp.logical_and(opens, step == 4))
        def _():
            pl.semaphore_wait(ready, len(answering))
            through = {(entry[0], entry[1]): entry for entry in passed if entry[2] == middle}
            for s in (0, 2):
                for half in range(2):
                    if (s, half) in through:
                        line_to_relay(through[s, half]).start()
                    else:
                        line_copy(s, half).start()

        for side in ("left", "right"):
            for late in (chunks - 2 * (heights - 1), step + AHEAD):
                first = isinstance(late, int)
                @pl.when(jnp.logical_and(
                    jnp.logical_and(relaying[side], late >= chunks - relay_count[side]),
                    step == 0 if first else late < chunks,
                ))
                def _(side=side, late=late):
                    for piece in range(2):
                        to_relay(side, late, piece).wait_recv()
                        from_relay(side, late, piece).start()

        @pl.when(step < chunks - 1)
        def _():
            add_lines(pl.ds(pl.multiple_of(HALF + c * CHUNK, CHUNK), CHUNK), 0, 5 * BLK,
                      pl.ds(pl.multiple_of(c * CHUNK, CHUNK), 5 * BLK))

    sent(chunks - 2, chunks)

    for s in range(4):
        @pl.when(has_before if s % 2 == 0 else has_after)
        def _(s=s):
            for half in range(2):
                line_copy(s, half).wait_send()

    @pl.loop(0, chunks)
    def _(step):
        for side in ("left", "right"):
            @pl.when(jnp.logical_and(relaying[side], step >= chunks - relay_count[side]))
            def _(side=side):
                for piece in range(2):
                    from_relay(side, step, piece).wait_send()

    for entry in passed:
        @pl.when(az == entry[3])
        def _(entry=entry):
            line_from_relay(entry).wait_send()


def finish(total, lines_in, azimuth_rows, out, stage, sems):
    lines, blocks = out.shape[1], azimuth_rows.shape[0]
    last = lines // 2
    start, stop = last - HALF, last + CHUNK + HALF
    copies = [
        pltpu.make_async_copy(total.at[:, HALF : HALF + start, :], out.at[:, 0:start, :], sems.at[0]),
        pltpu.make_async_copy(total.at[:, HALF + stop : HALF + lines, :], out.at[:, stop:lines, :], sems.at[1]),
    ]
    for copy in copies:
        copy.start()
    tiles = []
    for b in range(blocks):
        tile = lines_in[HALF + last : HALF + last + CHUNK, 2 * b * BLK : 2 * (b + 1) * BLK]
        real, imag = tile[:, :BLK], tile[:, BLK:]
        tiles.append(jnp.concatenate([tile, jnp.concatenate([imag, -real], axis=1)], axis=0))
    at = 0
    for piece, rows in enumerate((256, 256, 128)):
        for b in range(blocks):
            result = jnp.dot(azimuth_rows[b, at : at + rows, :], tiles[b], preferred_element_type=F32)
            columns = slice(b * BLK, (b + 1) * BLK)
            source = slice(HALF + start + at, HALF + start + at + rows)
            stage[0, at : at + rows, columns] = total[0, source, columns] + result[:, :BLK]
            stage[1, at : at + rows, columns] = total[1, source, columns] + result[:, BLK:]
        copy = pltpu.make_async_copy(
            stage.at[:, at : at + rows, :], out.at[:, start + at : start + at + rows, :], sems.at[2 + piece]
        )
        copy.start()
        copies.append(copy)
        at += rows
    for copy in copies:
        copy.wait()


def per_device(ranks, raw_echo, range_chirp, migration_taps, block_shift, azimuth_chirp):
    lines, cells = raw_echo.shape[1:]
    blocks = cells // BLK
    chunks = lines // CHUNK
    vmem = pl.BlockSpec(memory_space=pltpu.VMEM)
    hbm = pl.BlockSpec(memory_space=pltpu.HBM)
    total, migrated, azimuth_rows = pl.pallas_call(
        functools.partial(kernel, ranks),
        out_shape=(
            pltpu.VMEM((2, lines + 2 * HALF, cells), F32),
            pltpu.VMEM((lines + 2 * HALF, 2 * cells), BF16),
            pltpu.VMEM((blocks, 5 * BLK, 2 * BLK), BF16),
        ),
        in_specs=[hbm] * 5,
        out_specs=(vmem, vmem, vmem),
        scratch_shapes=[
            pltpu.VMEM((2, lines, cells), BF16),
            pltpu.VMEM((2, lines, HALF), BF16),
            pltpu.VMEM((2, lines, HALF), BF16),
            pltpu.VMEM((lines, BLK), BF16),
            pltpu.VMEM((lines, BLK), BF16),
            pltpu.VMEM((lines, BLK), BF16),
            pltpu.VMEM((lines, BLK), BF16),
            pltpu.VMEM((2, lines, HALF), BF16),
            pltpu.VMEM((lines, BLK), BF16),
            pltpu.VMEM((CHUNK // 2, 2 * cells), BF16),
            pltpu.VMEM((2, 6 * BLK, 2 * BLK), BF16),
            pltpu.VMEM((12 * BLK, 2 * BLK), BF16),
            pltpu.VMEM((blocks, 14 * BLK, 2 * BLK), BF16),
            pltpu.VMEM(range_chirp.shape, BF16),
            pltpu.VMEM(migration_taps.shape, BF16),
            pltpu.SMEM(block_shift.shape, jnp.int32),
            pltpu.VMEM(azimuth_chirp.shape, BF16),
            pltpu.SemaphoreType.DMA,
            pltpu.SemaphoreType.DMA((4,)),
            pltpu.SemaphoreType.DMA((2, 2, chunks)),
            pltpu.SemaphoreType.DMA((2, 2, chunks)),
            pltpu.SemaphoreType.DMA((4, 2)),
            pltpu.SemaphoreType.DMA((4, 2)),
            pltpu.SemaphoreType.DMA((2, chunks)),
            pltpu.SemaphoreType.DMA((2, chunks)),
            pltpu.SemaphoreType.DMA,
            pltpu.SemaphoreType.DMA,
            pltpu.SemaphoreType.REGULAR,
        ],
        compiler_params=pltpu.CompilerParams(collective_id=0, has_side_effects=True, vmem_limit_bytes=40 << 20),
        name="focus",
    )(*(
        pltpu.with_memory_space_constraint(value, pltpu.HBM)
        for value in (raw_echo, range_chirp, migration_taps, block_shift, azimuth_chirp)
    ))
    return pl.pallas_call(
        finish,
        out_shape=jax.ShapeDtypeStruct((2, lines, cells), F32),
        in_specs=[vmem, vmem, vmem],
        out_specs=hbm,
        scratch_shapes=[
            pltpu.VMEM((2, 2 * HALF + CHUNK, cells), F32),
            pltpu.SemaphoreType.DMA((5,)),
        ],
        compiler_params=pltpu.CompilerParams(vmem_limit_bytes=40 << 20),
        name="finish",
    )(total, migrated, azimuth_rows)


def solution(mesh):
    ranks = (mesh.shape["az"], mesh.shape["rg"])
    placed = (P(None, "az", "rg"), P(), P(None, "rg"), P("rg"), P("rg", None, None))
    return jax.shard_map(
        functools.partial(per_device, ranks), mesh=mesh, in_specs=placed, out_specs=P(None, "az", "rg"), check_vma=False
    )
```
